32 devices in a mesh: row: 4 (over y, x), col: 8 (over z, core).
Axes of the slice: x: 2, y: 2, z: 4, core: 2. Of those that a mesh axis runs over, the one named last changes fastest.
Arguments:
- features: bfloat16 [16384, 256], P(('row', 'col')), may hold values from -6 to 6
- weight: bfloat16 [256, 256], replicated, may hold values from -0.375 to 0.375
- bias_vector: float32 [256], replicated, may hold values from -3 to 3
- send_rows: int32 [4, 8, 8, 256], P('row', 'col'), may hold values from 0 to 511
- send_count: int32 [4, 8, 8], P('row', 'col'), may hold values from 1 to 256, as said below
- adjacency: bfloat16 [4, 8, 16, 16, 128, 128], P('row', 'col'), may hold values from 0 to 0.099609375
- source_tile: int32 [4, 8, 16, 16], P('row', 'col'), may hold values from 0 to 15, as said below
- tile_count: int32 [4, 8, 16], P('row', 'col'), may hold values from 1 to 16, as said below
- cotangent: bfloat16 [16384, 256], P(('row', 'col')), may hold values from -6 to 6
Outputs:
- output: bfloat16 [16384, 256], P(('row', 'col'))
- input_grad: bfloat16 [16384, 256], P(('row', 'col'))
- weight_grad: float32 [256, 256], replicated
- bias_grad: float32 [256], replicated
The draws below stay inside these ranges and needn't reach their ends.
Inputs may be any that keep to these rules, and one draw needn't show every extreme that they name: `send_rows`: rows of one list may repeat. `send_count`: in every grid row some grid column receives 256 rows from every piece of that grid row. `source_tile`: the 16 slots of one target tile read distinct boundary tiles. `tile_count`: slots at or beyond the count are ignored.
All inputs are finite; a program needn't handle non-finite values.
Results may differ from the reference program's by a relative error of at most 0.0063.
Values may be sent and summed in bfloat16 or wider, within the bound.
No kernel may reach another device: no remote copies, remote signals or barrier semaphores. Data moves between devices by JAX's collectives and lax.ppermute only.
A program may use at most 192 MiB of HBM per device.

```python
import math
import jax
import jax.numpy as jnp
from jax import lax

F = 256
TILE = 128
NODE_DEV = 512
SEND_TILES = 2
SLOTS = 16
GRID_ROWS = 4
GRID_COLS = 8
CAP = 256
TT = 16
ST = 16
NODES = 16384
N_ROW = 4
N_COL = 8


def draw_send_count(key, part):
    first_key, second_key = jax.random.split(key)
    counts = jax.random.randint(first_key, (N_ROW, N_COL, N_COL), 1, CAP + 1)
    full_column = jax.random.randint(second_key, (N_ROW, 1, 1), 0, N_COL)
    column_ids = jnp.arange(N_COL)[None, None, :]
    return jnp.where(column_ids == full_column, CAP, counts).astype(jnp.int32)


def draw_source_tile(key, part):
    scores = jax.random.randint(key, (N_ROW, N_COL, TT, ST), 0, 1 << 20)
    scores = scores * ST + jnp.arange(ST)[None, None, None, :]
    order = jnp.argsort(scores, axis=-1, stable=True)
    return order[..., :SLOTS].astype(jnp.int32)


def draw_tile_count(key, part):
    first_key, second_key, third_key = jax.random.split(key, 3)
    level = jax.random.randint(first_key, (N_ROW, N_COL, 1), 1, SLOTS + 1)
    counts = jax.random.randint(second_key, (N_ROW, N_COL, TT), 1, level + 1)
    chosen = jax.random.randint(third_key, (), 0, N_ROW * N_COL * TT)
    flat = counts.reshape(-1)
    flat = jnp.where(jnp.arange(N_ROW * N_COL * TT) == chosen, SLOTS, flat)
    return flat.reshape(N_ROW, N_COL, TT).astype(jnp.int32)


def place_ends(values, stream_key, low, high):
    dims = values.shape
    index_at = [jax.random.randint(jax.random.fold_in(stream_key, axis), (), 0, dims[axis]) for axis in range(len(dims))]
    values = values.at[tuple(index_at)].set(low)
    longest = dims.index(max(dims))
    index_at[longest] = (index_at[longest] + 1) % dims[longest]
    return values.at[tuple(index_at)].set(high)


def block_levels(own_key, extent, shards, least, high):
    loudness, own = 1.0, jax.random.fold_in(own_key, 6)
    for axis_at, blocks in shards:
        steps = jnp.exp(jax.random.uniform(jax.random.fold_in(own, axis_at), (blocks,), jnp.float32, least / len(shards), high / len(shards)))
        loudness = loudness * jnp.repeat(steps, extent[axis_at] // blocks).reshape([-1 if axis == axis_at else 1 for axis in range(len(extent))])
    return loudness


def gaussian(own_key, extent, spread, limit, shards=(), kind=jnp.bfloat16):
    values = jax.random.normal(own_key, extent, jnp.float32) * spread
    if len(shards) > 0:
        values = block_levels(own_key, extent, shards, -0.22, 0.18) * values
    return jnp.clip(values, min=-limit, max=limit).astype(kind)


def setup_inputs(seed: int = 0) -> dict:
    key_list = jax.random.split(jax.random.key(seed), 10)
    return {
        "features": gaussian(key_list[0], (NODES, F), 1.0, 6.0, ((0, 32),)),
        "weight": gaussian(key_list[1], (F, F), F ** -0.5, 0.375),
        "bias_vector": gaussian(key_list[2], (F,), 0.5, 3.0, (), jnp.float32),
        "send_rows": place_ends(jax.random.randint(key_list[3], (GRID_ROWS, GRID_COLS, GRID_COLS, CAP), 0, NODE_DEV), jax.random.fold_in(key_list[3], 1), 0, NODE_DEV - 1).astype(jnp.int32),
        "send_count": draw_send_count(jax.random.fold_in(key_list[9], 71), 0),
        "adjacency": jnp.clip(0.099609375 * jax.random.uniform(key_list[5], (GRID_ROWS, GRID_COLS, TT, SLOTS, TILE, TILE), jnp.float32) ** block_levels(key_list[5], (GRID_ROWS, GRID_COLS, TT, SLOTS, TILE, TILE), ((0, 4), (1, 8)), -0.2, 0.2), 0.0, 0.099609375).astype(jnp.bfloat16),
        "source_tile": draw_source_tile(jax.random.fold_in(key_list[9], 71), 0),
        "tile_count": draw_tile_count(jax.random.fold_in(key_list[9], 71), 0),
        "cotangent": gaussian(key_list[8], (NODES, F), 1.0, 6.0, ((0, 32),)),
    }


def boundary_block(features_row, list_rows, list_counts):
    picked = jax.vmap(lambda table, index: table[index])(features_row, list_rows)
    live_mask = jnp.arange(CAP)[None, :] < list_counts[:, None]
    picked = jnp.where(live_mask[:, :, None], picked, jnp.zeros((), picked.dtype))
    return picked.reshape(N_COL * SEND_TILES, TILE, F)

def live_tiles(tiles_here, slot_counts):
    live_mask = jnp.arange(SLOTS)[None, :] < slot_counts[:, None]
    return jnp.where(live_mask[:, :, None, None], tiles_here, jnp.zeros((), tiles_here.dtype))

def reference(features, weight, bias_vector, send_rows, send_count, adjacency, source_tile, tile_count, cotangent):
    target_tiles = N_ROW * NODE_DEV // TILE
    features_grid = features.reshape(N_ROW, N_COL, NODE_DEV, F)

    def column_sum(column):

        def cell(row_index):
            source_rows = boundary_block(features_grid[row_index], send_rows[row_index, :, column, :], send_count[row_index, :, column])
            tiles_here = live_tiles(adjacency[row_index, column], tile_count[row_index, column])
            gathered = source_rows[source_tile[row_index, column]]
            partial_value = jnp.einsum('tsab,tsbf->taf', tiles_here.astype(jnp.float32), gathered.astype(jnp.float32))
            return partial_value.reshape(target_tiles * TILE, F)
        parts = lax.map(cell, jnp.arange(N_ROW).astype(jnp.int32))
        return lax.optimization_barrier(jnp.sum(parts, axis=0))
    columns = lax.map(column_sum, jnp.arange(N_COL).astype(jnp.int32))
    summed = columns.reshape(N_COL, N_ROW, NODE_DEV, F).transpose(1, 0, 2, 3).reshape(NODES, F)
    aggregate = summed.astype(jnp.bfloat16)
    preact = jnp.dot(aggregate, weight, preferred_element_type=jnp.float32) + bias_vector
    output = jax.nn.silu(preact).astype(jnp.bfloat16)
    sigmoid_pre = jax.nn.sigmoid(preact)
    grad_pre = (cotangent.astype(jnp.float32) * sigmoid_pre * (1.0 + preact * (1.0 - sigmoid_pre))).astype(jnp.bfloat16)
    scale = 1.0 / math.sqrt(NODES)
    weight_grad = jnp.dot(aggregate.T, grad_pre, preferred_element_type=jnp.float32) * scale
    bias_grad = lax.optimization_barrier(jnp.sum(grad_pre.astype(jnp.float32), axis=0)) * scale
    back = jnp.dot(grad_pre, weight.T, preferred_element_type=jnp.float32).astype(jnp.bfloat16)
    back_grid = back.reshape(N_ROW, N_COL, NODE_DEV, F)

    def column_step(grad_grid, column):
        targets = back_grid[:, column].reshape(target_tiles, TILE, F)

        def cell(row_index):
            tiles_here = live_tiles(adjacency[row_index, column], tile_count[row_index, column])
            contrib = jnp.einsum('tsab,taf->tsbf', tiles_here.astype(jnp.float32), targets.astype(jnp.float32))
            index = source_tile[row_index, column].reshape(-1)
            gathered = jnp.zeros((N_COL * SEND_TILES, TILE, F), jnp.float32).at[index].add(contrib.reshape(target_tiles * SLOTS, TILE, F))
            gathered = gathered.reshape(N_COL, CAP, F)
            live_mask = jnp.arange(CAP)[None, :] < send_count[row_index, :, column][:, None]
            return jnp.where(live_mask[:, :, None], gathered, jnp.zeros((), jnp.float32))
        grads = lax.map(cell, jnp.arange(N_ROW).astype(jnp.int32))
        list_rows = send_rows[:, :, column, :]
        added = jax.vmap(jax.vmap(lambda table, index, values: table.at[index].add(values)))(grad_grid, list_rows, grads)
        return (added, None)
    grad_grid, _ = lax.scan(column_step, jnp.zeros((N_ROW, N_COL, NODE_DEV, F), jnp.float32), jnp.arange(N_COL).astype(jnp.int32))
    input_grad = grad_grid.reshape(NODES, F).astype(jnp.bfloat16)
    return (output, input_grad, weight_grad, bias_grad)
```

```python
import functools
import math

import jax
import jax.numpy as jnp
from jax import lax
from jax.experimental import pallas as pl
from jax.experimental.pallas import tpu as pltpu
from jax.sharding import PartitionSpec as P

TILE = 128
CHUNK = 128
VMEM_LIMIT = 40 * 1024 * 1024
BF16 = jnp.bfloat16
F32 = jnp.float32


def full_spec(shape):
    return pl.BlockSpec(shape, lambda *_: (0,) * len(shape))


def params(limit=VMEM_LIMIT):
    return pltpu.CompilerParams(vmem_limit_bytes=limit)


def xor_pairs(size, step):
    return [(i, i ^ step) for i in range(size)]


def z_pairs(pairs):
    return [(2 * a + core, 2 * b + core) for a, b in pairs for core in range(2)]


def densify_kernel(per_piece, src_ref, cnt_ref, pos_ref, adj_ref, out_ref):
    step = pl.program_id(0)
    tiles, slots = adj_ref.shape[0], adj_ref.shape[1]
    out_ref[...] = jnp.zeros_like(out_ref)
    here = pos_ref[1]
    for t in range(tiles):
        count = cnt_ref[step * tiles + t]
        for s in range(slots):

            @pl.when(s < count)
            def _(t=t, s=s):
                source = src_ref[step * tiles + t, s]
                slot = (source // per_piece) ^ here
                column = pl.multiple_of((slot * per_piece + source % per_piece) * TILE, TILE)
                out_ref[t * TILE : (t + 1) * TILE, pl.ds(column, TILE)] = adj_ref[t, s]


def densify(adjacency, source_tile, tile_count, pos, pieces, capacity):
    targets, slots = adjacency.shape[0], adjacency.shape[1]
    tiles = 4
    width = pieces * capacity
    return pl.pallas_call(
        functools.partial(densify_kernel, capacity // TILE),
        out_shape=jax.ShapeDtypeStruct((targets * TILE, width), BF16),
        grid_spec=pltpu.PrefetchScalarGridSpec(
            num_scalar_prefetch=3,
            grid=(targets // tiles,),
            in_specs=[pl.BlockSpec((tiles, slots, TILE, TILE), lambda i, *_: (i, 0, 0, 0))],
            out_specs=pl.BlockSpec((tiles * TILE, width), lambda i, *_: (i, 0)),
        ),
        compiler_params=params(),
        cost_estimate=pl.CostEstimate(
            flops=0, bytes_accessed=2 * targets * TILE * (width + slots * TILE), transcendentals=0
        ),
        name="densify",
    )(source_tile, tile_count, pos, adjacency)


def select_kernel(pos_ref, list_ref, pick_ref, put_ref):
    slot = pl.program_id(0)
    row = list_ref[pl.ds(slot ^ pos_ref[1], 1), :]
    nodes = put_ref.shape[1]
    hit = lax.broadcasted_iota(jnp.int32, (nodes, row.shape[1]), 0) == row
    put = jnp.where(hit, 1.0, 0.0).astype(BF16)
    put_ref[0] = put
    pick_ref[0] = put.T


def selectors(lists, pos, nodes):
    pieces, capacity = lists.shape
    return pl.pallas_call(
        select_kernel,
        out_shape=(
            jax.ShapeDtypeStruct((pieces, capacity, nodes), BF16),
            jax.ShapeDtypeStruct((pieces, nodes, capacity), BF16),
        ),
        grid_spec=pltpu.PrefetchScalarGridSpec(
            num_scalar_prefetch=1,
            grid=(pieces,),
            in_specs=[pl.BlockSpec((pieces, capacity), lambda i, *_: (0, 0))],
            out_specs=(
                pl.BlockSpec((1, capacity, nodes), lambda i, *_: (i, 0, 0)),
                pl.BlockSpec((1, nodes, capacity), lambda i, *_: (i, 0, 0)),
            ),
        ),
        compiler_params=params(),
        cost_estimate=pl.CostEstimate(
            flops=0, bytes_accessed=4 * pieces * capacity * nodes, transcendentals=0
        ),
        name="selectors",
    )(pos, lists)


def forward_kernel(groups, peers, pos_ref, pick_ref, dense_ref, *rest):
    total = sum(groups)
    sources, outs, gathered = rest[:total], rest[total : total + peers], rest[total + peers]
    step = pl.program_id(0)
    capacity = pick_ref.shape[1]

    @pl.when(step == 0)
    def _():
        at = 0
        for slot, count in enumerate(groups):
            piece = sources[at][...]
            for extra in range(1, count):
                piece = piece + sources[at + extra][...]
            at += count
            rows = jnp.dot(pick_ref[slot], piece, preferred_element_type=F32)
            gathered[slot * capacity : (slot + 1) * capacity, :] = rows.astype(BF16)

    result = jnp.dot(dense_ref[...], gathered[...], preferred_element_type=F32)
    for peer in range(peers):

        @pl.when(step == peer)
        def _(peer=peer):
            outs[peer][...] = result.astype(outs[peer].dtype)


def forward(dense, pick, groups, pos, peers):
    rows, width = dense.shape
    flat = [array for group in groups for array in group]
    nodes, chunk = flat[0].shape
    block = rows // peers
    return pl.pallas_call(
        functools.partial(forward_kernel, tuple(len(group) for group in groups), peers),
        out_shape=tuple(
            jax.ShapeDtypeStruct((block, chunk), F32 if peer == 0 else BF16)
            for peer in range(peers)
        ),
        grid_spec=pltpu.PrefetchScalarGridSpec(
            num_scalar_prefetch=1,
            grid=(peers,),
            in_specs=[
                full_spec(pick.shape),
                pl.BlockSpec((block, width), lambda i, pos_ref: (i ^ pos_ref[0], 0)),
            ]
            + [full_spec((nodes, chunk))] * len(flat),
            out_specs=tuple(full_spec((block, chunk)) for _ in range(peers)),
            scratch_shapes=[pltpu.VMEM((width, chunk), BF16)],
        ),
        compiler_params=params(),
        cost_estimate=pl.CostEstimate(
            flops=2 * rows * width * chunk, bytes_accessed=2 * rows * width, transcendentals=0
        ),
        name="forward_rows",
    )(pos, pick, dense, *flat)


def layer_kernel(chunks, peers, weight_ref, bias_ref, cot_ref, *rest):
    parts, outs = rest[: chunks * peers], rest[chunks * peers :]
    out_ref, agg_ref, grad_ref = outs[:3]
    columns = []
    for chunk in range(chunks):
        total = parts[chunk * peers][...].astype(F32)
        for peer in range(1, peers):
            total = total + parts[chunk * peers + peer][...].astype(F32)
        columns.append(total.astype(BF16))
    agg = jnp.concatenate(columns, axis=1) if chunks > 1 else columns[0]
    weight = weight_ref[...]
    preact = jnp.dot(agg, weight, preferred_element_type=F32) + bias_ref[...]
    sigma = 1.0 / (1.0 + jnp.exp(-preact))
    out_ref[...] = (preact * sigma).astype(BF16)
    grad = (cot_ref[...].astype(F32) * sigma * (1.0 + preact * (1.0 - sigma))).astype(BF16)
    agg_ref[...] = agg
    grad_ref[...] = grad
    back = lax.dot_general(
        weight, grad, (((1,), (1,)), ((), ())), preferred_element_type=F32
    ).astype(BF16)
    size = weight.shape[0] // chunks
    for chunk in range(chunks):
        outs[3 + chunk][...] = back[chunk * size : (chunk + 1) * size, :]


def layer(weight, bias_vector, cotangent, parts, chunks, peers):
    nodes, width = cotangent.shape
    size = width // chunks
    return pl.pallas_call(
        functools.partial(layer_kernel, chunks, peers),
        out_shape=(jax.ShapeDtypeStruct((nodes, width), BF16),) * 3
        + (jax.ShapeDtypeStruct((size, nodes), BF16),) * chunks,
        compiler_params=params(),
        cost_estimate=pl.CostEstimate(
            flops=4 * nodes * width * width,
            bytes_accessed=2 * nodes * width * 10,
            transcendentals=nodes * width,
        ),
        name="layer",
    )(weight, bias_vector.reshape(1, -1), cotangent, *parts)


def weights_kernel(agg_ref, grad_ref, top_ref, low_ref, bias_ref):
    grad = grad_ref[...]
    product = lax.dot_general(
        agg_ref[...], grad, (((0,), (0,)), ((), ())), preferred_element_type=F32
    )
    half = top_ref.shape[0]
    top_ref[...] = product[:half]
    low_ref[...] = product[half:]
    bias_ref[...] = jnp.sum(grad.astype(F32).reshape(-1, 8, grad.shape[1]), axis=0)


def weight_partials(agg, grad):
    nodes, width = agg.shape
    return pl.pallas_call(
        weights_kernel,
        out_shape=(
            jax.ShapeDtypeStruct((width // 2, width), F32),
            jax.ShapeDtypeStruct((width // 2, width), F32),
            jax.ShapeDtypeStruct((8, width), F32),
        ),
        compiler_params=params(),
        cost_estimate=pl.CostEstimate(
            flops=2 * nodes * width * width, bytes_accessed=6 * nodes * width, transcendentals=0
        ),
        name="weight_partials",
    )(agg, grad)


def backward_kernel(peers, slots, kept, pos_ref, put_ref, dense_ref, *rest):
    backs, outs, total = rest[:peers], rest[peers : peers + slots], rest[peers + slots]
    step = pl.program_id(0)
    capacity = put_ref.shape[2]
    for peer in range(peers):

        @pl.when(step == peer)
        def _(peer=peer):
            product = jnp.dot(backs[peer][...], dense_ref[...], preferred_element_type=F32)
            if peer == 0:
                total[...] = product
            else:
                total[...] += product

    @pl.when(step == peers - 1)
    def _():
        for slot in range(slots):
            rows = total[:, slot * capacity : (slot + 1) * capacity].astype(BF16)
            outs[slot][...] = lax.dot_general(
                put_ref[slot], rows, (((1,), (1,)), ((), ())), preferred_element_type=F32
            ).astype(outs[slot].dtype)


def backward(dense, put, backs, pos, kept):
    peers = len(backs)
    rows, width = dense.shape
    slots, nodes, _ = put.shape
    chunk = backs[0].shape[0]
    block = rows // peers
    return pl.pallas_call(
        functools.partial(backward_kernel, peers, slots, kept),
        out_shape=tuple(
            jax.ShapeDtypeStruct((nodes, chunk), F32 if slot in kept else BF16)
            for slot in range(slots)
        ),
        grid_spec=pltpu.PrefetchScalarGridSpec(
            num_scalar_prefetch=1,
            grid=(peers,),
            in_specs=[
                full_spec(put.shape),
                pl.BlockSpec((block, width), lambda i, pos_ref: (i ^ pos_ref[0], 0)),
            ]
            + [full_spec((chunk, block))] * peers,
            out_specs=tuple(full_spec((nodes, chunk)) for _ in range(slots)),
            scratch_shapes=[pltpu.VMEM((chunk, width), F32)],
        ),
        compiler_params=params(),
        cost_estimate=pl.CostEstimate(
            flops=2 * rows * width * chunk, bytes_accessed=2 * rows * width, transcendentals=0
        ),
        name="backward_rows",
    )(pos, put, dense, *backs)


def pair_sum_kernel(count, *refs):
    for i in range(count):
        total = refs[i][...].astype(F32) + refs[count + i][...].astype(F32)
        refs[2 * count + i][...] = total.astype(refs[2 * count + i].dtype)


def pair_sums(kept, received):
    count = len(kept)
    return pl.pallas_call(
        functools.partial(pair_sum_kernel, count),
        out_shape=tuple(
            jax.ShapeDtypeStruct(kept[i].shape, F32 if i == 0 else BF16) for i in range(count)
        ),
        compiler_params=params(),
        cost_estimate=pl.CostEstimate(
            flops=0, bytes_accessed=count * kept[0].size * 8, transcendentals=0
        ),
        name="pair_sums",
    )(*kept, *received)


def finish_kernel(chunks, each, *refs):
    out_ref = refs[-1]
    size = out_ref.shape[1] // chunks
    for chunk in range(chunks):
        total = refs[chunk * each][...].astype(F32)
        for term in range(1, each):
            total = total + refs[chunk * each + term][...].astype(F32)
        out_ref[:, chunk * size : (chunk + 1) * size] = total.astype(BF16)


def finish(terms):
    chunks, each = len(terms), len(terms[0])
    nodes, size = terms[0][0].shape
    return pl.pallas_call(
        functools.partial(finish_kernel, chunks, each),
        out_shape=jax.ShapeDtypeStruct((nodes, size * chunks), BF16),
        compiler_params=params(),
        cost_estimate=pl.CostEstimate(
            flops=0, bytes_accessed=chunks * nodes * size * 2 * each, transcendentals=0
        ),
        name="finish",
    )(*[array for group in terms for array in group])


LINE_SWAP1 = z_pairs([(0, 1), (1, 0), (2, 3), (3, 2)])
LINE_SWAP2 = z_pairs([(0, 2), (2, 0), (1, 3), (3, 1)])
LINE_MIDDLE = z_pairs([(1, 2), (2, 1)])
LINE_OUT = z_pairs([(2, 3), (1, 0)])
LINE_IN = z_pairs([(3, 2), (0, 1)])
CORE = xor_pairs(8, 1)


def spread(piece, columns):
    if columns != 8:
        return [[piece]] + [
            [lax.ppermute(piece, "col", xor_pairs(columns, step))] for step in range(1, columns)
        ]
    far = lax.ppermute(piece, "col", LINE_SWAP2)
    near = lax.ppermute(piece, "col", LINE_SWAP1)
    middle = lax.ppermute(piece, "col", LINE_MIDDLE)
    ends = lax.ppermute(far, "col", LINE_OUT)
    own = [[piece], [near], [far], [middle, ends]]
    other = [[lax.ppermute(a, "col", CORE) for a in group] for group in own]
    return [group for pair in zip(own, other) for group in pair]


def collect(pieces, columns):
    if columns != 8:
        return [pieces[0]] + [
            lax.ppermute(pieces[step], "col", xor_pairs(columns, step))
            for step in range(1, columns)
        ]
    received = [lax.ppermute(pieces[2 * z + 1], "col", CORE) for z in range(4)]
    own, near, far, last = pair_sums([pieces[2 * z] for z in range(4)], received)
    passed = lax.ppermute(last, "col", LINE_IN)
    middle = lax.ppermute(last, "col", LINE_MIDDLE)
    from_near = lax.ppermute(near, "col", LINE_SWAP1)
    far = (far.astype(F32) + passed.astype(F32)).astype(BF16)
    from_far = lax.ppermute(far, "col", LINE_SWAP2)
    return [own, middle, from_near, from_far]


def sum_everywhere(top, low, bias, rows, columns):
    core = lax.axis_index("col") % 2
    mine = jnp.where(core == 0, top, low)
    theirs = jnp.where(core == 0, low, top)
    mine = mine + lax.ppermute(theirs, "col", xor_pairs(columns, 1))
    bias = bias + lax.ppermute(bias, "col", xor_pairs(columns, 1))
    both = jnp.concatenate([mine, bias], axis=0)
    step = 2
    while step < columns:
        both = both + lax.ppermute(both, "col", xor_pairs(columns, step))
        step *= 2
    step = 1
    while step < rows:
        both = both + lax.ppermute(both, "row", xor_pairs(rows, step))
        step *= 2
    mine = both[: mine.shape[0]]
    theirs = lax.ppermute(mine, "col", xor_pairs(columns, 1))
    weight_sum = jnp.concatenate(
        [jnp.where(core == 0, mine, theirs), jnp.where(core == 0, theirs, mine)], axis=0
    )
    return weight_sum, jnp.sum(both[mine.shape[0] :], axis=0)


def per_device(
    features,
    weight,
    bias_vector,
    send_rows,
    send_count,
    adjacency,
    source_tile,
    tile_count,
    cotangent,
):
    rows, columns = lax.axis_size("row"), lax.axis_size("col")
    nodes, width = features.shape
    list_rows, list_counts = send_rows[0, 0], send_count[0, 0]
    capacity = list_rows.shape[1]
    chunks = width // CHUNK
    pos = jnp.stack([lax.axis_index("row"), lax.axis_index("col")]).astype(jnp.int32)

    slots = [
        spread(features[:, chunk * CHUNK : (chunk + 1) * CHUNK], columns)
        for chunk in range(chunks)
    ]
    live = jnp.arange(capacity)[None, :] < list_counts[:, None]
    lists = lax.all_to_all(
        jnp.where(live, list_rows, -1), "col", split_axis=0, concat_axis=0, tiled=True
    )
    dense = densify(adjacency[0, 0], source_tile[0, 0], tile_count[0, 0], pos, columns, capacity)
    pick, put = selectors(lists, pos, nodes)

    parts = []
    for chunk in range(chunks):
        blocks = forward(dense, pick, slots[chunk], pos, rows)
        parts.append(blocks[0])
        for step in range(1, rows):
            parts.append(lax.ppermute(blocks[step], "row", xor_pairs(rows, step)))

    results = layer(weight, bias_vector, cotangent, parts, chunks, rows)
    output, agg, grad_pre = results[:3]
    backs = [
        [back] + [lax.ppermute(back, "row", xor_pairs(rows, step)) for step in range(1, rows)]
        for back in results[3:]
    ]
    top, low, bias = weight_partials(agg, grad_pre)
    weight_sum, bias_sum = sum_everywhere(top, low, bias, rows, columns)
    scale = 1.0 / math.sqrt(nodes * rows * columns)

    kept = tuple(range(0, columns, 2)) if columns == 8 else (0,)
    terms = [
        collect(backward(dense, put, backs[chunk], pos, kept), columns)
        for chunk in range(chunks)
    ]
    return output, finish(terms), weight_sum * scale, bias_sum * scale


def solution(mesh):
    in_specs = (
        P(("row", "col"), None),
        P(),
        P(),
        P("row", "col", None, None),
        P("row", "col", None),
        P("row", "col", None, None, None, None),
        P("row", "col", None, None),
        P("row", "col", None),
        P(("row", "col"), None),
    )
    out_specs = (P(("row", "col"), None), P(("row", "col"), None), P(), P())
    return jax.shard_map(
        per_device, mesh=mesh, in_specs=in_specs, out_specs=out_specs, check_vma=False
    )
```

```python
import functools
import math

import jax
import jax.numpy as jnp
from jax import lax
from jax.experimental import pallas as pl
from jax.experimental.pallas import tpu as pltpu
from jax.sharding import PartitionSpec as P

TILE = 128
VMEM_LIMIT = 16 * 1024 * 1024
BIG_LIMIT = 40 * 1024 * 1024
RESIDENT = 16 * 1024 * 1024
BF16 = jnp.bfloat16
F32 = jnp.float32


def full_spec(shape):
    return pl.BlockSpec(shape, lambda *_: (0,) * len(shape))


def params(limit=VMEM_LIMIT):
    return pltpu.CompilerParams(vmem_limit_bytes=limit)


def xor_pairs(size, step):
    return [(i, i ^ step) for i in range(size)]


def z_pairs(pairs):
    return [(2 * a + core, 2 * b + core) for a, b in pairs for core in range(2)]


def densify_kernel(per_piece, per_peer, src_ref, cnt_ref, pos_ref, adj_ref, out_ref, held, sems):
    targets, slots = adj_ref.shape[0], adj_ref.shape[1]
    here = pos_ref[1]
    whole = slots * TILE == out_ref.shape[1]
    copies = [
        pltpu.make_async_copy(adj_ref.at[t], held.at[t], sems.at[t]) for t in range(targets)
    ]
    for copy in copies:
        copy.start()
    for t, copy in enumerate(copies):
        place = ((t // per_peer) ^ pos_ref[0]) * per_peer + t % per_peer
        rows = pl.ds(pl.multiple_of(place * TILE, TILE), TILE)
        if not whole:
            out_ref[rows, :] = jnp.zeros((TILE, out_ref.shape[1]), out_ref.dtype)
        count = cnt_ref[t]
        copy.wait()
        for s in range(slots):
            source = src_ref[t, s]
            slot = (source // per_piece) ^ here
            column = pl.multiple_of((slot * per_piece + source % per_piece) * TILE, TILE)
            tile = held[t, s]
            out_ref[rows, pl.ds(column, TILE)] = jnp.where(s < count, tile, jnp.zeros_like(tile))


def densify(adjacency, source_tile, tile_count, pos, peers, pieces, capacity):
    targets = adjacency.shape[0]
    width = pieces * capacity
    smem = pl.BlockSpec(memory_space=pltpu.SMEM)
    return pl.pallas_call(
        functools.partial(densify_kernel, capacity // TILE, targets // peers),
        out_shape=jax.ShapeDtypeStruct((targets * TILE, width), BF16),
        in_specs=[smem, smem, smem, pl.BlockSpec(memory_space=pl.ANY)],
        out_specs=pl.BlockSpec(memory_space=pltpu.VMEM),
        scratch_shapes=[
            pltpu.VMEM(adjacency.shape, BF16),
            pltpu.SemaphoreType.DMA((targets,)),
        ],
        compiler_params=params(40 * 1024 * 1024),
        cost_estimate=pl.CostEstimate(
            flops=0, bytes_accessed=4 * targets * TILE * width, transcendentals=0
        ),
        name="densify",
    )(source_tile, tile_count, pos, adjacency)


def densify_blocks_kernel(per_piece, src_ref, cnt_ref, pos_ref, adj_ref, out_ref):
    step = pl.program_id(0)
    tiles, slots = adj_ref.shape[0], adj_ref.shape[1]
    out_ref[...] = jnp.zeros_like(out_ref)
    here = pos_ref[1]
    for t in range(tiles):
        count = cnt_ref[step * tiles + t]
        for s in range(slots):

            @pl.when(s < count)
            def _(t=t, s=s):
                source = src_ref[step * tiles + t, s]
                slot = (source // per_piece) ^ here
                column = pl.multiple_of((slot * per_piece + source % per_piece) * TILE, TILE)
                out_ref[t * TILE : (t + 1) * TILE, pl.ds(column, TILE)] = adj_ref[t, s]


def densify_blocks(adjacency, source_tile, tile_count, pos, pieces, capacity):
    targets, slots = adjacency.shape[0], adjacency.shape[1]
    tiles = 4
    width = pieces * capacity
    return pl.pallas_call(
        functools.partial(densify_blocks_kernel, capacity // TILE),
        out_shape=jax.ShapeDtypeStruct((targets * TILE, width), BF16),
        grid_spec=pltpu.PrefetchScalarGridSpec(
            num_scalar_prefetch=3,
            grid=(targets // tiles,),
            in_specs=[pl.BlockSpec((tiles, slots, TILE, TILE), lambda i, *_: (i, 0, 0, 0))],
            out_specs=pl.BlockSpec((tiles * TILE, width), lambda i, *_: (i, 0)),
        ),
        compiler_params=params(BIG_LIMIT),
        cost_estimate=pl.CostEstimate(
            flops=0, bytes_accessed=2 * targets * TILE * (width + slots * TILE), transcendentals=0
        ),
        name="densify",
    )(source_tile, tile_count, pos, adjacency)


def hits(row, nodes):
    node = lax.broadcasted_iota(jnp.int32, (nodes, row.shape[1]), 0).astype(F32)
    return jnp.where(node == row, 1.0, 0.0).astype(BF16)


def list_row(high, low):
    return high.astype(F32) * 256.0 + low.astype(F32)


def select_kernel(list_ref, pick_ref, put_ref):
    slots, nodes, _ = put_ref.shape
    for slot in range(slots):
        put = hits(list_ref[slot : slot + 1, :], nodes)
        put_ref[slot] = put
        pick_ref[slot] = put.T


def selectors(lists, nodes):
    pieces, capacity = lists.shape
    return pl.pallas_call(
        select_kernel,
        out_shape=(
            jax.ShapeDtypeStruct((pieces, capacity, nodes), BF16),
            jax.ShapeDtypeStruct((pieces, nodes, capacity), BF16),
        ),
        compiler_params=params(BIG_LIMIT),
        cost_estimate=pl.CostEstimate(
            flops=0, bytes_accessed=4 * pieces * capacity * nodes, transcendentals=0
        ),
        name="selectors",
    )(lists)


def gather_rows(sources, here, put_ref, at):
    nodes, capacity = put_ref.shape[1:]
    columns = (sources[0].shape[0] - nodes) // 2
    piece = sources[0][:nodes, :]
    tail = sources[0][nodes:, :].astype(F32)
    for extra in sources[1:]:
        piece = piece + extra[:nodes, :]
        tail = tail + extra[nodes:, :].astype(F32)
    table = list_row(tail[:columns], tail[columns:])
    mine = lax.broadcasted_iota(jnp.int32, table.shape, 0) == here
    put = hits(jnp.sum(jnp.where(mine, table, 0.0), axis=0, keepdims=True), nodes)
    put_ref[at] = put
    rows = lax.dot_general(put, piece, (((0,), (0,)), ((), ())), preferred_element_type=F32)
    return rows.astype(BF16)


def forward_part_kernel(groups, base, peers, last, pos_ref, dense_ref, *rest):
    total = sum(groups)
    sources, rest = rest[:total], rest[total:]
    if last:
        partial_ref, outs, put_ref, gathered = rest[0], rest[1 : 1 + peers], rest[1 + peers], rest[-1]
    else:
        partial_ref, put_ref, gathered = rest
    here = pos_ref[1]
    capacity = put_ref.shape[2]
    at = 0
    for slot, count in enumerate(groups):
        rows = gather_rows(sources[at : at + count], here, put_ref, slot)
        gathered[slot * capacity : (slot + 1) * capacity, :] = rows
        at += count
    columns = slice(base * capacity, (base + len(groups)) * capacity)
    if not last:
        partial_ref[...] = jnp.dot(
            dense_ref[:, columns], gathered[...], preferred_element_type=F32
        )
        return
    block = outs[0].shape[0]
    for peer in range(peers):
        here_rows = slice(peer * block, (peer + 1) * block)
        result = partial_ref[here_rows, :] + jnp.dot(
            dense_ref[here_rows, columns], gathered[...], preferred_element_type=F32
        )
        outs[peer][...] = result.astype(outs[peer].dtype)


def forward_part(dense, groups, base, pos, peers, nodes, capacity, before=None):
    rows = dense.shape[0]
    flat = [array for group in groups for array in group]
    width = flat[0].shape[1]
    last = before is not None
    put = jax.ShapeDtypeStruct((len(groups), nodes, capacity), BF16)
    if last:
        outs = tuple(
            jax.ShapeDtypeStruct((rows // peers, width), F32 if peer == 0 else BF16)
            for peer in range(peers)
        ) + (put,)
        flat = flat + [before]
    else:
        outs = (jax.ShapeDtypeStruct((rows, width), F32), put)
    depth = len(groups) * capacity
    return pl.pallas_call(
        functools.partial(
            forward_part_kernel, tuple(len(group) for group in groups), base, peers, last
        ),
        out_shape=outs,
        in_specs=[pl.BlockSpec(memory_space=pltpu.SMEM)]
        + [pl.BlockSpec(memory_space=pltpu.VMEM)] * (1 + len(flat)),
        scratch_shapes=[pltpu.VMEM((depth, width), BF16)],
        compiler_params=params(),
        cost_estimate=pl.CostEstimate(
            flops=2 * rows * depth * width, bytes_accessed=2 * rows * depth, transcendentals=0
        ),
        name="forward_late" if last else "forward_early",
    )(pos, dense, *flat)


def forward_blocks_kernel(groups, peers, pos_ref, pick_ref, dense_ref, *rest):
    total = sum(groups)
    sources, outs, gathered = rest[:total], rest[total : total + peers], rest[total + peers]
    step = pl.program_id(0)
    capacity = pick_ref.shape[1]

    @pl.when(step == 0)
    def _():
        at = 0
        for slot, count in enumerate(groups):
            piece = sources[at][...]
            for extra in range(1, count):
                piece = piece + sources[at + extra][...]
            at += count
            rows = jnp.dot(pick_ref[slot], piece, preferred_element_type=F32)
            gathered[slot * capacity : (slot + 1) * capacity, :] = rows.astype(BF16)

    result = jnp.dot(dense_ref[...], gathered[...], preferred_element_type=F32)
    for peer in range(peers):

        @pl.when(step == peer)
        def _(peer=peer):
            outs[peer][...] = result.astype(outs[peer].dtype)


def forward_blocks(dense, pick, groups, pos, peers):
    rows, width = dense.shape
    flat = [array for group in groups for array in group]
    nodes, chunk = flat[0].shape
    block = rows // peers
    return pl.pallas_call(
        functools.partial(forward_blocks_kernel, tuple(len(group) for group in groups), peers),
        out_shape=tuple(
            jax.ShapeDtypeStruct((block, chunk), F32 if peer == 0 else BF16)
            for peer in range(peers)
        ),
        grid_spec=pltpu.PrefetchScalarGridSpec(
            num_scalar_prefetch=1,
            grid=(peers,),
            in_specs=[
                full_spec(pick.shape),
                pl.BlockSpec((block, width), lambda i, pos_ref: (i ^ pos_ref[0], 0)),
            ]
            + [full_spec((nodes, chunk))] * len(flat),
            out_specs=tuple(full_spec((block, chunk)) for _ in range(peers)),
            scratch_shapes=[pltpu.VMEM((width, chunk), BF16)],
        ),
        compiler_params=params(BIG_LIMIT),
        cost_estimate=pl.CostEstimate(
            flops=2 * rows * width * chunk, bytes_accessed=2 * rows * width, transcendentals=0
        ),
        name="forward_rows",
    )(pos, pick, dense, *flat)


def layer_kernel(peers, weight_ref, bias_ref, cot_ref, *rest):
    parts, outs = rest[:peers], rest[peers:]
    out_ref, agg_ref, grad_ref = outs[:3]
    total = parts[0][...].astype(F32)
    for peer in range(1, peers):
        total = total + parts[peer][...].astype(F32)
    agg = total.astype(BF16)
    weight = weight_ref[...]
    preact = jnp.dot(agg, weight, preferred_element_type=F32) + bias_ref[...]
    sigma = 1.0 / (1.0 + jnp.exp(-preact))
    out_ref[...] = (preact * sigma).astype(BF16)
    grad = (cot_ref[...].astype(F32) * sigma * (1.0 + preact * (1.0 - sigma))).astype(BF16)
    agg_ref[...] = agg
    grad_ref[...] = grad
    outs[3][...] = lax.dot_general(
        grad, weight, (((1,), (1,)), ((), ())), preferred_element_type=F32
    ).astype(BF16)


def layer(weight, bias_vector, cotangent, parts):
    nodes, width = cotangent.shape
    return pl.pallas_call(
        functools.partial(layer_kernel, len(parts)),
        out_shape=(jax.ShapeDtypeStruct((nodes, width), BF16),) * 4,
        compiler_params=params(),
        cost_estimate=pl.CostEstimate(
            flops=4 * nodes * width * width,
            bytes_accessed=2 * nodes * width * 10,
            transcendentals=nodes * width,
        ),
        name="layer",
    )(weight, bias_vector.reshape(1, -1), cotangent, *parts)


def weights_kernel(scale, pos_ref, agg_ref, grad_ref, mine_ref, theirs_ref):
    grad = grad_ref[...]
    product = scale * lax.dot_general(
        agg_ref[...], grad, (((0,), (0,)), ((), ())), preferred_element_type=F32
    )
    bias = scale * jnp.sum(grad.astype(F32).reshape(-1, 8, grad.shape[1]), axis=0)
    half = product.shape[0] // 2
    core = pos_ref[1] % 2
    for keep, give, parity in ((mine_ref, theirs_ref, 0), (theirs_ref, mine_ref, 1)):

        @pl.when(core == parity)
        def _(keep=keep, give=give):
            keep[:half] = product[:half]
            give[:half] = product[half:]

    mine_ref[half:] = bias
    theirs_ref[half:] = bias


def weight_partials(agg, grad, pos, scale):
    nodes, width = agg.shape
    return pl.pallas_call(
        functools.partial(weights_kernel, scale),
        out_shape=(jax.ShapeDtypeStruct((width // 2 + 8, width), F32),) * 2,
        in_specs=[pl.BlockSpec(memory_space=pltpu.SMEM)]
        + [pl.BlockSpec(memory_space=pltpu.VMEM)] * 2,
        compiler_params=params(),
        cost_estimate=pl.CostEstimate(
            flops=2 * nodes * width * width, bytes_accessed=6 * nodes * width, transcendentals=0
        ),
        name="weight_partials",
    )(pos, agg, grad)


def assemble_kernel(pos_ref, mine_ref, theirs_ref, weight_ref, bias_ref):
    half = weight_ref.shape[0] // 2
    core = pos_ref[1] % 2
    mine = pl.multiple_of(core * half, half)
    theirs = pl.multiple_of((1 - core) * half, half)
    weight_ref[pl.ds(mine, half), :] = mine_ref[:half]
    weight_ref[pl.ds(theirs, half), :] = theirs_ref[:half]
    bias_ref[...] = jnp.sum(mine_ref[half:], axis=0, keepdims=True)


def assemble(mine, theirs, pos):
    width = mine.shape[1]
    weight, bias = pl.pallas_call(
        assemble_kernel,
        out_shape=(
            jax.ShapeDtypeStruct((width, width), F32),
            jax.ShapeDtypeStruct((1, width), F32),
        ),
        in_specs=[pl.BlockSpec(memory_space=pltpu.SMEM)]
        + [pl.BlockSpec(memory_space=pltpu.VMEM)] * 2,
        compiler_params=params(),
        cost_estimate=pl.CostEstimate(
            flops=0, bytes_accessed=16 * width * width, transcendentals=0
        ),
        name="assemble",
    )(pos, mine, theirs)
    return weight, bias.reshape(width)


def back_product(dense, back):
    return lax.dot_general(
        dense, back, (((0,), (0,)), ((), ())), preferred_element_type=F32
    )


def backward_early_kernel(dense_ref, back_ref, out_ref):
    out_ref[...] = back_product(dense_ref[: back_ref.shape[0], :], back_ref[...])


def backward_early(dense, back):
    width, size = dense.shape[1], back.shape[1]
    return pl.pallas_call(
        backward_early_kernel,
        out_shape=jax.ShapeDtypeStruct((width, size), F32),
        compiler_params=params(),
        cost_estimate=pl.CostEstimate(
            flops=2 * width * back.size, bytes_accessed=6 * width * size, transcendentals=0
        ),
        name="backward_early",
    )(dense, back)


def backward_late_kernel(base, slots, peers, dense_ref, put_ref, first_ref, *rest):
    backs, outs, (joined, rows) = rest[: peers - 1], rest[peers - 1 : -2], rest[-2:]
    capacity = put_ref.shape[2]
    block = backs[0].shape[0]
    for peer in range(1, peers):
        joined[(peer - 1) * block : peer * block, :] = backs[peer - 1][...]
    columns = slice(base * capacity, (base + slots) * capacity)
    rows[...] = (
        first_ref[columns, :] + back_product(dense_ref[block:, columns], joined[...])
    ).astype(BF16)
    for slot in range(slots):
        outs[slot][...] = jnp.dot(
            put_ref[slot],
            rows[slot * capacity : (slot + 1) * capacity, :],
            preferred_element_type=F32,
        ).astype(outs[slot].dtype)


def backward_late(dense, put, first, backs, base):
    slots, nodes, capacity = put.shape
    size = first.shape[1]
    return pl.pallas_call(
        functools.partial(backward_late_kernel, base, slots, len(backs) + 1),
        out_shape=tuple(
            jax.ShapeDtypeStruct((nodes, size), BF16 if slot % 2 else F32)
            for slot in range(slots)
        ),
        scratch_shapes=[
            pltpu.VMEM((len(backs) * backs[0].shape[0], size), BF16),
            pltpu.VMEM((slots * capacity, size), BF16),
        ],
        compiler_params=params(),
        cost_estimate=pl.CostEstimate(
            flops=2 * slots * capacity * size * dense.shape[0],
            bytes_accessed=2 * dense.shape[0] * slots * capacity,
            transcendentals=0,
        ),
        name="backward_late",
    )(dense, put, first, *backs)


def backward_blocks_kernel(peers, slots, pos_ref, put_ref, dense_ref, *rest):
    backs, outs, total = rest[:peers], rest[peers : peers + slots], rest[peers + slots]
    step = pl.program_id(0)
    capacity = put_ref.shape[2]
    for peer in range(peers):

        @pl.when(step == peer)
        def _(peer=peer):
            product = lax.dot_general(
                dense_ref[...], backs[peer][...], (((0,), (0,)), ((), ())), preferred_element_type=F32
            )
            if peer == 0:
                total[...] = product
            else:
                total[...] += product

    @pl.when(step == peers - 1)
    def _():
        for slot in range(slots):
            rows = total[slot * capacity : (slot + 1) * capacity, :].astype(BF16)
            outs[slot][...] = jnp.dot(put_ref[slot], rows, preferred_element_type=F32).astype(
                outs[slot].dtype
            )


def backward_blocks(dense, put, backs, pos, kept):
    peers = len(backs)
    rows, width = dense.shape
    slots, nodes, _ = put.shape
    chunk = backs[0].shape[1]
    block = rows // peers
    return pl.pallas_call(
        functools.partial(backward_blocks_kernel, peers, slots),
        out_shape=tuple(
            jax.ShapeDtypeStruct((nodes, chunk), F32 if slot in kept else BF16)
            for slot in range(slots)
        ),
        grid_spec=pltpu.PrefetchScalarGridSpec(
            num_scalar_prefetch=1,
            grid=(peers,),
            in_specs=[
                full_spec(put.shape),
                pl.BlockSpec((block, width), lambda i, pos_ref: (i ^ pos_ref[0], 0)),
            ]
            + [full_spec((block, chunk))] * peers,
            out_specs=tuple(full_spec((nodes, chunk)) for _ in range(slots)),
            scratch_shapes=[pltpu.VMEM((width, chunk), F32)],
        ),
        compiler_params=params(BIG_LIMIT),
        cost_estimate=pl.CostEstimate(
            flops=2 * rows * width * chunk, bytes_accessed=2 * rows * width, transcendentals=0
        ),
        name="backward_rows",
    )(pos, put, dense, *backs)


def pair_sum_kernel(count, *refs):
    for i in range(count):
        total = refs[i][...].astype(F32) + refs[count + i][...].astype(F32)
        refs[2 * count + i][...] = total.astype(refs[2 * count + i].dtype)


def pair_sums(kept, received, wide=-1):
    count = len(kept)
    return pl.pallas_call(
        functools.partial(pair_sum_kernel, count),
        out_shape=tuple(
            jax.ShapeDtypeStruct(kept[i].shape, F32 if i == wide else BF16) for i in range(count)
        ),
        compiler_params=params(),
        cost_estimate=pl.CostEstimate(
            flops=0, bytes_accessed=count * kept[0].size * 8, transcendentals=0
        ),
        name="pair_sums",
    )(*kept, *received)


def finish_kernel(chunks, each, *refs):
    out_ref = refs[-1]
    size = out_ref.shape[1] // chunks
    for chunk in range(chunks):
        total = refs[chunk * each][...].astype(F32)
        for term in range(1, each):
            total = total + refs[chunk * each + term][...].astype(F32)
        out_ref[:, chunk * size : (chunk + 1) * size] = total.astype(BF16)


def finish(terms):
    chunks, each = len(terms), len(terms[0])
    nodes, size = terms[0][0].shape
    return pl.pallas_call(
        functools.partial(finish_kernel, chunks, each),
        out_shape=jax.ShapeDtypeStruct((nodes, size * chunks), BF16),
        compiler_params=params(),
        cost_estimate=pl.CostEstimate(
            flops=0, bytes_accessed=chunks * nodes * size * 2 * each, transcendentals=0
        ),
        name="finish",
    )(*[array for group in terms for array in group])


LINE_SWAP1 = z_pairs([(0, 1), (1, 0), (2, 3), (3, 2)])
LINE_SWAP2 = z_pairs([(0, 2), (2, 0), (1, 3), (3, 1)])
LINE_MIDDLE = z_pairs([(1, 2), (2, 1)])
LINE_OUT = z_pairs([(2, 3), (1, 0)])
LINE_IN = z_pairs([(3, 2), (0, 1)])
CORE = xor_pairs(8, 1)


def after(value, *others):
    return lax.optimization_barrier((value,) + others)[0]


def exchange_add(value, axis, size, step):
    return value + lax.ppermute(value, axis, xor_pairs(size, step))


def with_lists(features, list_rows, list_counts):
    live = jnp.arange(list_rows.shape[1])[None, :] < list_counts[:, None]
    high = jnp.where(live, list_rows // 256, -1)
    low = jnp.where(live, list_rows % 256, 0)
    return jnp.concatenate([features, high.astype(BF16), low.astype(BF16)], axis=0)


def line_exchange(piece, dense_of, pos, nodes, capacity, rows):
    far = lax.ppermute(piece, "col", LINE_SWAP2)
    near = lax.ppermute(piece, "col", LINE_SWAP1)
    other = lax.ppermute(piece, "col", CORE)
    dense = dense_of()
    far, dense = lax.optimization_barrier((far, dense))
    ends = lax.ppermute(far, "col", LINE_OUT)
    middle = lax.ppermute(after(piece, far), "col", LINE_MIDDLE)
    early = [[piece], [other], [near], [lax.ppermute(near, "col", CORE)], [far]]
    early.append([lax.ppermute(far, "col", CORE)])
    partial, put_early = forward_part(dense, early, 0, pos, rows, nodes, capacity)
    partial, middle, ends = lax.optimization_barrier((partial, middle, ends))
    late = [[middle, ends], [lax.ppermute(middle, "col", CORE), lax.ppermute(ends, "col", CORE)]]
    *blocks, put_late = forward_part(dense, late, 6, pos, rows, nodes, capacity, partial)
    return dense, put_early, put_late, blocks


def row_exchange(own, arrays, rows):
    received = [
        lax.ppermute(arrays[step - 1], "row", xor_pairs(rows, step))
        for step in reversed(range(1, rows))
    ]
    return [own] + received[::-1]


def line_reduce(dense, put_early, put_late, back, backs, pos, sums, rows, columns):
    first = backward_early(dense, back)
    sums = exchange_add(sums, "col", columns, 2)
    sums = exchange_add(sums, "col", columns, 4)
    *backs, first, sums = lax.optimization_barrier((*backs, first, sums))
    keep3, give3 = backward_late(dense, put_late, first, backs, 6)
    got3 = lax.ppermute(give3, "col", CORE)
    sums = exchange_add(sums, "row", rows, 1)
    keep0, give0, keep1, give1, keep2, give2 = backward_late(dense, put_early, first, backs, 0)
    got3, give2, give1, give0, keep0, sums = lax.optimization_barrier(
        (got3, give2, give1, give0, keep0, sums)
    )
    step = 2
    while step < rows:
        sums = exchange_add(sums, "row", rows, step)
        step *= 2
    (last,) = pair_sums([keep3], [got3])
    passed = lax.ppermute(last, "col", LINE_IN)
    middle = lax.ppermute(last, "col", LINE_MIDDLE)
    got = [lax.ppermute(give, "col", CORE) for give in (give0, give1, give2)]
    own, near, far = pair_sums([keep0, keep1, keep2], got, 0)
    passed, middle, sums = lax.optimization_barrier((passed, middle, sums))
    far = (far.astype(F32) + passed.astype(F32)).astype(BF16)
    from_far = lax.ppermute(far, "col", LINE_SWAP2)
    from_near = lax.ppermute(after(near, far), "col", LINE_SWAP1)
    return [own, middle, from_near, from_far], sums


def per_device(
    features,
    weight,
    bias_vector,
    send_rows,
    send_count,
    adjacency,
    source_tile,
    tile_count,
    cotangent,
):
    rows, columns = lax.axis_size("row"), lax.axis_size("col")
    nodes, width = features.shape
    capacity = send_rows.shape[3]
    tiles, source, count = adjacency[0, 0], source_tile[0, 0], tile_count[0, 0]
    pos = jnp.stack([lax.axis_index("row"), lax.axis_index("col")]).astype(jnp.int32)
    piece = with_lists(features, send_rows[0, 0], send_count[0, 0])
    line = columns == 8 and 2 * tiles.shape[0] * TILE * columns * capacity <= RESIDENT

    if line:
        dense, put_early, put_late, blocks = line_exchange(
            piece,
            lambda: densify(tiles, source, count, pos, rows, columns, capacity),
            pos,
            nodes,
            capacity,
            rows,
        )
    else:
        dense = densify_blocks(tiles, source, count, pos, columns, capacity)
        pieces = [piece] + [
            lax.ppermute(piece, "col", xor_pairs(columns, step)) for step in range(1, columns)
        ]
        here = lax.axis_index("col")
        lists = jnp.stack(
            [
                list_row(
                    lax.dynamic_index_in_dim(a, nodes + here, 0, keepdims=False),
                    lax.dynamic_index_in_dim(a, nodes + columns + here, 0, keepdims=False),
                )
                for a in pieces
            ]
        )
        pick, put = selectors(lists, nodes)
        blocks = forward_blocks(dense, pick, [[a[:nodes]] for a in pieces], pos, rows)

    parts = row_exchange(blocks[0], blocks[1:], rows)
    output, agg, grad_pre, back = layer(weight, bias_vector, cotangent, parts)
    backs = row_exchange(back, [back] * (rows - 1), rows)
    scale = 1.0 / math.sqrt(nodes * rows * columns)
    mine, theirs = weight_partials(agg, grad_pre, pos, scale)
    sums = mine + lax.ppermute(theirs, "col", CORE if line else xor_pairs(columns, 1))

    if line:
        terms, sums = line_reduce(
            dense, put_early, put_late, back, backs[1:], pos, sums, rows, columns
        )
    else:
        scattered = backward_blocks(dense, put, backs, pos, (0,))
        terms = [scattered[0]] + [
            lax.ppermute(scattered[step], "col", xor_pairs(columns, step))
            for step in range(1, columns)
        ]
        step = 2
        while step < columns:
            sums = exchange_add(sums, "col", columns, step)
            step *= 2
        step = 1
        while step < rows:
            sums = exchange_add(sums, "row", rows, step)
            step *= 2
    weight_grad, bias_grad = assemble(
        sums, lax.ppermute(sums, "col", xor_pairs(columns, 1)), pos
    )
    terms[-2], weight_grad, bias_grad = lax.optimization_barrier(
        (terms[-2], weight_grad, bias_grad)
    )
    return output, finish([terms]), weight_grad, bias_grad


def solution(mesh):
    in_specs = (
        P(("row", "col"), None),
        P(),
        P(),
        P("row", "col", None, None),
        P("row", "col", None),
        P("row", "col", None, None, None, None),
        P("row", "col", None, None),
        P("row", "col", None),
        P(("row", "col"), None),
    )
    out_specs = (P(("row", "col"), None), P(("row", "col"), None), P(), P())
    return jax.shard_map(
        per_device, mesh=mesh, in_specs=in_specs, out_specs=out_specs, check_vma=False
    )
```

```python
import functools
import math

import jax
import jax.numpy as jnp
from jax import lax
from jax.experimental import pallas as pl
from jax.experimental.pallas import tpu as pltpu
from jax.sharding import PartitionSpec as P

TILE = 128
VMEM_LIMIT = 16 * 1024 * 1024
BIG_LIMIT = 40 * 1024 * 1024
RESIDENT = 16 * 1024 * 1024
BF16 = jnp.bfloat16
F32 = jnp.float32


def full_spec(shape):
    return pl.BlockSpec(shape, lambda *_: (0,) * len(shape))


def params(limit=VMEM_LIMIT):
    return pltpu.CompilerParams(vmem_limit_bytes=limit)


def xor_pairs(size, step):
    return [(i, i ^ step) for i in range(size)]


def z_pairs(pairs):
    return [(2 * a + core, 2 * b + core) for a, b in pairs for core in range(2)]


def densify_kernel(per_piece, per_peer, src_ref, cnt_ref, pos_ref, adj_ref, out_ref, held, sems):
    targets, slots = adj_ref.shape[0], adj_ref.shape[1]
    here = pos_ref[1]
    whole = slots * TILE == out_ref.shape[1]
    copies = [
        pltpu.make_async_copy(adj_ref.at[t], held.at[t], sems.at[t]) for t in range(targets)
    ]
    for copy in copies:
        copy.start()
    for t, copy in enumerate(copies):
        place = ((t // per_peer) ^ pos_ref[0]) * per_peer + t % per_peer
        rows = pl.ds(pl.multiple_of(place * TILE, TILE), TILE)
        if not whole:
            out_ref[rows, :] = jnp.zeros((TILE, out_ref.shape[1]), out_ref.dtype)
        count = cnt_ref[t]
        copy.wait()
        for s in range(slots):
            source = src_ref[t, s]
            slot = (source // per_piece) ^ here
            column = pl.multiple_of((slot * per_piece + source % per_piece) * TILE, TILE)
            tile = held[t, s]
            out_ref[rows, pl.ds(column, TILE)] = jnp.where(s < count, tile, jnp.zeros_like(tile))


def densify(adjacency, source_tile, tile_count, pos, peers, pieces, capacity):
    targets = adjacency.shape[0]
    width = pieces * capacity
    smem = pl.BlockSpec(memory_space=pltpu.SMEM)
    return pl.pallas_call(
        functools.partial(densify_kernel, capacity // TILE, targets // peers),
        out_shape=jax.ShapeDtypeStruct((targets * TILE, width), BF16),
        in_specs=[smem, smem, smem, pl.BlockSpec(memory_space=pl.ANY)],
        out_specs=pl.BlockSpec(memory_space=pltpu.VMEM),
        scratch_shapes=[
            pltpu.VMEM(adjacency.shape, BF16),
            pltpu.SemaphoreType.DMA((targets,)),
        ],
        compiler_params=params(40 * 1024 * 1024),
        cost_estimate=pl.CostEstimate(
            flops=0, bytes_accessed=4 * targets * TILE * width, transcendentals=0
        ),
        name="densify",
    )(source_tile, tile_count, pos, adjacency)


def densify_blocks_kernel(per_piece, src_ref, cnt_ref, pos_ref, adj_ref, out_ref):
    step = pl.program_id(0)
    tiles, slots = adj_ref.shape[0], adj_ref.shape[1]
    out_ref[...] = jnp.zeros_like(out_ref)
    here = pos_ref[1]
    for t in range(tiles):
        count = cnt_ref[step * tiles + t]
        for s in range(slots):

            @pl.when(s < count)
            def _(t=t, s=s):
                source = src_ref[step * tiles + t, s]
                slot = (source // per_piece) ^ here
                column = pl.multiple_of((slot * per_piece + source % per_piece) * TILE, TILE)
                out_ref[t * TILE : (t + 1) * TILE, pl.ds(column, TILE)] = adj_ref[t, s]


def densify_blocks(adjacency, source_tile, tile_count, pos, pieces, capacity):
    targets, slots = adjacency.shape[0], adjacency.shape[1]
    tiles = 4
    width = pieces * capacity
    return pl.pallas_call(
        functools.partial(densify_blocks_kernel, capacity // TILE),
        out_shape=jax.ShapeDtypeStruct((targets * TILE, width), BF16),
        grid_spec=pltpu.PrefetchScalarGridSpec(
            num_scalar_prefetch=3,
            grid=(targets // tiles,),
            in_specs=[pl.BlockSpec((tiles, slots, TILE, TILE), lambda i, *_: (i, 0, 0, 0))],
            out_specs=pl.BlockSpec((tiles * TILE, width), lambda i, *_: (i, 0)),
        ),
        compiler_params=params(BIG_LIMIT),
        cost_estimate=pl.CostEstimate(
            flops=0, bytes_accessed=2 * targets * TILE * (width + slots * TILE), transcendentals=0
        ),
        name="densify",
    )(source_tile, tile_count, pos, adjacency)


def hits(row, nodes):
    node = lax.broadcasted_iota(jnp.int32, (nodes, row.shape[1]), 0).astype(F32)
    return jnp.where(node == row, 1.0, 0.0).astype(BF16)


def list_row(high, low):
    return high.astype(F32) * 256.0 + low.astype(F32)


def select_kernel(list_ref, pick_ref, put_ref):
    slots, nodes, _ = put_ref.shape
    for slot in range(slots):
        put = hits(list_ref[slot : slot + 1, :], nodes)
        put_ref[slot] = put
        pick_ref[slot] = put.T


def selectors(lists, nodes):
    pieces, capacity = lists.shape
    return pl.pallas_call(
        select_kernel,
        out_shape=(
            jax.ShapeDtypeStruct((pieces, capacity, nodes), BF16),
            jax.ShapeDtypeStruct((pieces, nodes, capacity), BF16),
        ),
        compiler_params=params(BIG_LIMIT),
        cost_estimate=pl.CostEstimate(
            flops=0, bytes_accessed=4 * pieces * capacity * nodes, transcendentals=0
        ),
        name="selectors",
    )(lists)


def gather_rows(sources, here, put_ref, at):
    nodes, capacity = put_ref.shape[1:]
    columns = (sources[0].shape[0] - nodes) // 2
    piece = sources[0][:nodes, :]
    tail = sources[0][nodes:, :].astype(F32)
    for extra in sources[1:]:
        piece = piece + extra[:nodes, :]
        tail = tail + extra[nodes:, :].astype(F32)
    table = list_row(tail[:columns], tail[columns:])
    mine = lax.broadcasted_iota(jnp.int32, table.shape, 0) == here
    put = hits(jnp.sum(jnp.where(mine, table, 0.0), axis=0, keepdims=True), nodes)
    put_ref[at] = put
    rows = lax.dot_general(put, piece, (((0,), (0,)), ((), ())), preferred_element_type=F32)
    return rows.astype(BF16)


def forward_part_kernel(groups, base, peers, last, pos_ref, dense_ref, *rest):
    total = sum(groups)
    sources, rest = rest[:total], rest[total:]
    if last:
        partial_ref, outs, put_ref, gathered = rest[0], rest[1 : 1 + peers], rest[1 + peers], rest[-1]
    else:
        partial_ref, put_ref, gathered = rest
    here = pos_ref[1]
    capacity = put_ref.shape[2]
    at = 0
    for slot, count in enumerate(groups):
        rows = gather_rows(sources[at : at + count], here, put_ref, slot)
        gathered[slot * capacity : (slot + 1) * capacity, :] = rows
        at += count
    columns = slice(base * capacity, (base + len(groups)) * capacity)
    if not last:
        partial_ref[...] = jnp.dot(
            dense_ref[:, columns], gathered[...], preferred_element_type=F32
        )
        return
    block = outs[0].shape[0]
    for peer in range(peers):
        here_rows = slice(peer * block, (peer + 1) * block)
        result = partial_ref[here_rows, :] + jnp.dot(
            dense_ref[here_rows, columns], gathered[...], preferred_element_type=F32
        )
        outs[peer][...] = result.astype(outs[peer].dtype)


def forward_part(dense, groups, base, pos, peers, nodes, capacity, before=None):
    rows = dense.shape[0]
    flat = [array for group in groups for array in group]
    width = flat[0].shape[1]
    last = before is not None
    put = jax.ShapeDtypeStruct((len(groups), nodes, capacity), BF16)
    if last:
        outs = tuple(
            jax.ShapeDtypeStruct((rows // peers, width), F32 if peer == 0 else BF16)
            for peer in range(peers)
        ) + (put,)
        flat = flat + [before]
    else:
        outs = (jax.ShapeDtypeStruct((rows, width), F32), put)
    depth = len(groups) * capacity
    return pl.pallas_call(
        functools.partial(
            forward_part_kernel, tuple(len(group) for group in groups), base, peers, last
        ),
        out_shape=outs,
        in_specs=[pl.BlockSpec(memory_space=pltpu.SMEM)]
        + [pl.BlockSpec(memory_space=pltpu.VMEM)] * (1 + len(flat)),
        scratch_shapes=[pltpu.VMEM((depth, width), BF16)],
        compiler_params=params(),
        cost_estimate=pl.CostEstimate(
            flops=2 * rows * depth * width, bytes_accessed=2 * rows * depth, transcendentals=0
        ),
        name="forward_late" if last else "forward_early",
    )(pos, dense, *flat)


def forward_blocks_kernel(groups, peers, pos_ref, pick_ref, dense_ref, *rest):
    total = sum(groups)
    sources, outs, gathered = rest[:total], rest[total : total + peers], rest[total + peers]
    step = pl.program_id(0)
    capacity = pick_ref.shape[1]

    @pl.when(step == 0)
    def _():
        at = 0
        for slot, count in enumerate(groups):
            piece = sources[at][...]
            for extra in range(1, count):
                piece = piece + sources[at + extra][...]
            at += count
            rows = jnp.dot(pick_ref[slot], piece, preferred_element_type=F32)
            gathered[slot * capacity : (slot + 1) * capacity, :] = rows.astype(BF16)

    result = jnp.dot(dense_ref[...], gathered[...], preferred_element_type=F32)
    for peer in range(peers):

        @pl.when(step == peer)
        def _(peer=peer):
            outs[peer][...] = result.astype(outs[peer].dtype)


def forward_blocks(dense, pick, groups, pos, peers):
    rows, width = dense.shape
    flat = [array for group in groups for array in group]
    nodes, chunk = flat[0].shape
    block = rows // peers
    return pl.pallas_call(
        functools.partial(forward_blocks_kernel, tuple(len(group) for group in groups), peers),
        out_shape=tuple(
            jax.ShapeDtypeStruct((block, chunk), F32 if peer == 0 else BF16)
            for peer in range(peers)
        ),
        grid_spec=pltpu.PrefetchScalarGridSpec(
            num_scalar_prefetch=1,
            grid=(peers,),
            in_specs=[
                full_spec(pick.shape),
                pl.BlockSpec((block, width), lambda i, pos_ref: (i ^ pos_ref[0], 0)),
            ]
            + [full_spec((nodes, chunk))] * len(flat),
            out_specs=tuple(full_spec((block, chunk)) for _ in range(peers)),
            scratch_shapes=[pltpu.VMEM((width, chunk), BF16)],
        ),
        compiler_params=params(BIG_LIMIT),
        cost_estimate=pl.CostEstimate(
            flops=2 * rows * width * chunk, bytes_accessed=2 * rows * width, transcendentals=0
        ),
        name="forward_rows",
    )(pos, pick, dense, *flat)


def layer_kernel(peers, weight_ref, bias_ref, cot_ref, *rest):
    parts, outs = rest[:peers], rest[peers:]
    out_ref, agg_ref, grad_ref = outs[:3]
    total = parts[0][...].astype(F32)
    for peer in range(1, peers):
        total = total + parts[peer][...].astype(F32)
    agg = total.astype(BF16)
    weight = weight_ref[...]
    preact = jnp.dot(agg, weight, preferred_element_type=F32) + bias_ref[...]
    sigma = 1.0 / (1.0 + jnp.exp(-preact))
    out_ref[...] = (preact * sigma).astype(BF16)
    grad = (cot_ref[...].astype(F32) * sigma * (1.0 + preact * (1.0 - sigma))).astype(BF16)
    agg_ref[...] = agg
    grad_ref[...] = grad
    outs[3][...] = lax.dot_general(
        grad, weight, (((1,), (1,)), ((), ())), preferred_element_type=F32
    ).astype(BF16)


def layer(weight, bias_vector, cotangent, parts):
    nodes, width = cotangent.shape
    return pl.pallas_call(
        functools.partial(layer_kernel, len(parts)),
        out_shape=(jax.ShapeDtypeStruct((nodes, width), BF16),) * 4,
        compiler_params=params(),
        cost_estimate=pl.CostEstimate(
            flops=4 * nodes * width * width,
            bytes_accessed=2 * nodes * width * 10,
            transcendentals=nodes * width,
        ),
        name="layer",
    )(weight, bias_vector.reshape(1, -1), cotangent, *parts)


def weights_kernel(scale, pos_ref, agg_ref, grad_ref, mine_ref, theirs_ref):
    grad = grad_ref[...]
    product = scale * lax.dot_general(
        agg_ref[...], grad, (((0,), (0,)), ((), ())), preferred_element_type=F32
    )
    bias = scale * jnp.sum(grad.astype(F32).reshape(-1, 8, grad.shape[1]), axis=0)
    half = product.shape[0] // 2
    core = pos_ref[1] % 2
    for keep, give, parity in ((mine_ref, theirs_ref, 0), (theirs_ref, mine_ref, 1)):

        @pl.when(core == parity)
        def _(keep=keep, give=give):
            keep[:half] = product[:half]
            give[:half] = product[half:]

    mine_ref[half:] = bias
    theirs_ref[half:] = bias


def weight_partials(agg, grad, pos, scale):
    nodes, width = agg.shape
    return pl.pallas_call(
        functools.partial(weights_kernel, scale),
        out_shape=(jax.ShapeDtypeStruct((width // 2 + 8, width), F32),) * 2,
        in_specs=[pl.BlockSpec(memory_space=pltpu.SMEM)]
        + [pl.BlockSpec(memory_space=pltpu.VMEM)] * 2,
        compiler_params=params(),
        cost_estimate=pl.CostEstimate(
            flops=2 * nodes * width * width, bytes_accessed=6 * nodes * width, transcendentals=0
        ),
        name="weight_partials",
    )(pos, agg, grad)


def assemble_kernel(pos_ref, mine_ref, theirs_ref, weight_ref, bias_ref):
    half = weight_ref.shape[0] // 2
    core = pos_ref[1] % 2
    mine = pl.multiple_of(core * half, half)
    theirs = pl.multiple_of((1 - core) * half, half)
    weight_ref[pl.ds(mine, half), :] = mine_ref[:half]
    weight_ref[pl.ds(theirs, half), :] = theirs_ref[:half]
    bias_ref[...] = jnp.sum(mine_ref[half:], axis=0, keepdims=True)


def assemble(mine, theirs, pos):
    width = mine.shape[1]
    weight, bias = pl.pallas_call(
        assemble_kernel,
        out_shape=(
            jax.ShapeDtypeStruct((width, width), F32),
            jax.ShapeDtypeStruct((1, width), F32),
        ),
        in_specs=[pl.BlockSpec(memory_space=pltpu.SMEM)]
        + [pl.BlockSpec(memory_space=pltpu.VMEM)] * 2,
        compiler_params=params(),
        cost_estimate=pl.CostEstimate(
            flops=0, bytes_accessed=16 * width * width, transcendentals=0
        ),
        name="assemble",
    )(pos, mine, theirs)
    return weight, bias.reshape(width)


def back_product(dense, back):
    return lax.dot_general(
        dense, back, (((0,), (0,)), ((), ())), preferred_element_type=F32
    )


def backward_early_kernel(dense_ref, back_ref, out_ref):
    out_ref[...] = back_product(dense_ref[: back_ref.shape[0], :], back_ref[...])


def backward_early(dense, back):
    width, size = dense.shape[1], back.shape[1]
    return pl.pallas_call(
        backward_early_kernel,
        out_shape=jax.ShapeDtypeStruct((width, size), F32),
        compiler_params=params(),
        cost_estimate=pl.CostEstimate(
            flops=2 * width * back.size, bytes_accessed=6 * width * size, transcendentals=0
        ),
        name="backward_early",
    )(dense, back)


def backward_late_kernel(base, slots, peers, dense_ref, put_ref, first_ref, *rest):
    backs, outs, (joined, rows) = rest[: peers - 1], rest[peers - 1 : -2], rest[-2:]
    capacity = put_ref.shape[2]
    block = backs[0].shape[0]
    for peer in range(1, peers):
        joined[(peer - 1) * block : peer * block, :] = backs[peer - 1][...]
    columns = slice(base * capacity, (base + slots) * capacity)
    rows[...] = (
        first_ref[columns, :] + back_product(dense_ref[block:, columns], joined[...])
    ).astype(BF16)
    for slot in range(slots):
        outs[slot][...] = jnp.dot(
            put_ref[slot],
            rows[slot * capacity : (slot + 1) * capacity, :],
            preferred_element_type=F32,
        ).astype(outs[slot].dtype)


def backward_late(dense, put, first, backs, base):
    slots, nodes, capacity = put.shape
    size = first.shape[1]
    return pl.pallas_call(
        functools.partial(backward_late_kernel, base, slots, len(backs) + 1),
        out_shape=tuple(
            jax.ShapeDtypeStruct((nodes, size), BF16 if slot % 2 else F32)
            for slot in range(slots)
        ),
        scratch_shapes=[
            pltpu.VMEM((len(backs) * backs[0].shape[0], size), BF16),
            pltpu.VMEM((slots * capacity, size), BF16),
        ],
        compiler_params=params(),
        cost_estimate=pl.CostEstimate(
            flops=2 * slots * capacity * size * dense.shape[0],
            bytes_accessed=2 * dense.shape[0] * slots * capacity,
            transcendentals=0,
        ),
        name="backward_late",
    )(dense, put, first, *backs)


def backward_blocks_kernel(peers, slots, pos_ref, put_ref, dense_ref, *rest):
    backs, outs, total = rest[:peers], rest[peers : peers + slots], rest[peers + slots]
    step = pl.program_id(0)
    capacity = put_ref.shape[2]
    for peer in range(peers):

        @pl.when(step == peer)
        def _(peer=peer):
            product = lax.dot_general(
                dense_ref[...], backs[peer][...], (((0,), (0,)), ((), ())), preferred_element_type=F32
            )
            if peer == 0:
                total[...] = product
            else:
                total[...] += product

    @pl.when(step == peers - 1)
    def _():
        for slot in range(slots):
            rows = total[slot * capacity : (slot + 1) * capacity, :].astype(BF16)
            outs[slot][...] = jnp.dot(put_ref[slot], rows, preferred_element_type=F32).astype(
                outs[slot].dtype
            )


def backward_blocks(dense, put, backs, pos, kept):
    peers = len(backs)
    rows, width = dense.shape
    slots, nodes, _ = put.shape
    chunk = backs[0].shape[1]
    block = rows // peers
    return pl.pallas_call(
        functools.partial(backward_blocks_kernel, peers, slots),
        out_shape=tuple(
            jax.ShapeDtypeStruct((nodes, chunk), F32 if slot in kept else BF16)
            for slot in range(slots)
        ),
        grid_spec=pltpu.PrefetchScalarGridSpec(
            num_scalar_prefetch=1,
            grid=(peers,),
            in_specs=[
                full_spec(put.shape),
                pl.BlockSpec((block, width), lambda i, pos_ref: (i ^ pos_ref[0], 0)),
            ]
            + [full_spec((block, chunk))] * peers,
            out_specs=tuple(full_spec((nodes, chunk)) for _ in range(slots)),
            scratch_shapes=[pltpu.VMEM((width, chunk), F32)],
        ),
        compiler_params=params(BIG_LIMIT),
        cost_estimate=pl.CostEstimate(
            flops=2 * rows * width * chunk, bytes_accessed=2 * rows * width, transcendentals=0
        ),
        name="backward_rows",
    )(pos, put, dense, *backs)


def pair_sum_kernel(count, *refs):
    for i in range(count):
        total = refs[i][...].astype(F32) + refs[count + i][...].astype(F32)
        refs[2 * count + i][...] = total.astype(refs[2 * count + i].dtype)


def pair_sums(kept, received, wide=-1):
    count = len(kept)
    return pl.pallas_call(
        functools.partial(pair_sum_kernel, count),
        out_shape=tuple(
            jax.ShapeDtypeStruct(kept[i].shape, F32 if i == wide else BF16) for i in range(count)
        ),
        compiler_params=params(),
        cost_estimate=pl.CostEstimate(
            flops=0, bytes_accessed=count * kept[0].size * 8, transcendentals=0
        ),
        name="pair_sums",
    )(*kept, *received)


def finish_kernel(chunks, each, *refs):
    out_ref = refs[-1]
    size = out_ref.shape[1] // chunks
    for chunk in range(chunks):
        total = refs[chunk * each][...].astype(F32)
        for term in range(1, each):
            total = total + refs[chunk * each + term][...].astype(F32)
        out_ref[:, chunk * size : (chunk + 1) * size] = total.astype(BF16)


def finish(terms):
    chunks, each = len(terms), len(terms[0])
    nodes, size = terms[0][0].shape
    return pl.pallas_call(
        functools.partial(finish_kernel, chunks, each),
        out_shape=jax.ShapeDtypeStruct((nodes, size * chunks), BF16),
        compiler_params=params(),
        cost_estimate=pl.CostEstimate(
            flops=0, bytes_accessed=chunks * nodes * size * 2 * each, transcendentals=0
        ),
        name="finish",
    )(*[array for group in terms for array in group])


LINE_SWAP1 = z_pairs([(0, 1), (1, 0), (2, 3), (3, 2)])
LINE_SWAP2 = z_pairs([(0, 2), (2, 0), (1, 3), (3, 1)])
LINE_MIDDLE = z_pairs([(1, 2), (2, 1)])
LINE_OUT = z_pairs([(2, 3), (1, 0)])
LINE_IN = z_pairs([(3, 2), (0, 1)])
CORE = xor_pairs(8, 1)


def after(value, *others):
    return lax.optimization_barrier((value,) + others)[0]


def exchange_add(value, axis, size, step):
    return value + lax.ppermute(value, axis, xor_pairs(size, step))


def with_lists(features, list_rows, list_counts):
    live = jnp.arange(list_rows.shape[1])[None, :] < list_counts[:, None]
    high = jnp.where(live, list_rows // 256, -1)
    low = jnp.where(live, list_rows % 256, 0)
    return jnp.concatenate([features, high.astype(BF16), low.astype(BF16)], axis=0)


def line_exchange(piece, dense_of, pos, nodes, capacity, rows):
    far = lax.ppermute(piece, "col", LINE_SWAP2)
    near = lax.ppermute(piece, "col", LINE_SWAP1)
    other = lax.ppermute(piece, "col", CORE)
    dense = dense_of()
    far, dense = lax.optimization_barrier((far, dense))
    ends = lax.ppermute(far, "col", LINE_OUT)
    middle = lax.ppermute(after(piece, far), "col", LINE_MIDDLE)
    early = [[piece], [other], [near], [lax.ppermute(near, "col", CORE)], [far]]
    early.append([lax.ppermute(far, "col", CORE)])
    partial, put_early = forward_part(dense, early, 0, pos, rows, nodes, capacity)
    partial, middle, ends = lax.optimization_barrier((partial, middle, ends))
    late = [[middle, ends], [lax.ppermute(middle, "col", CORE), lax.ppermute(ends, "col", CORE)]]
    *blocks, put_late = forward_part(dense, late, 6, pos, rows, nodes, capacity, partial)
    return dense, put_early, put_late, blocks


def row_exchange(own, arrays, rows):
    received = [
        lax.ppermute(arrays[step - 1], "row", xor_pairs(rows, step))
        for step in reversed(range(1, rows))
    ]
    return [own] + received[::-1]


def line_reduce(dense, put_early, put_late, back, backs, pos, sums, rows, columns):
    first = backward_early(dense, back)
    sums = exchange_add(sums, "col", columns, 2)
    sums = exchange_add(sums, "col", columns, 4)
    *backs, first, sums = lax.optimization_barrier((*backs, first, sums))
    keep3, give3 = backward_late(dense, put_late, first, backs, 6)
    got3 = lax.ppermute(give3, "col", CORE)
    received = lax.ppermute(sums, "row", xor_pairs(rows, 1))
    keep0, give0, keep1, give1, keep2, give2 = backward_late(dense, put_early, first, backs, 0)
    got3, give2, give1, give0, keep0 = lax.optimization_barrier((got3, give2, give1, give0, keep0))
    (last,) = pair_sums([keep3], [got3])
    passed = lax.ppermute(last, "col", LINE_IN)
    middle = lax.ppermute(last, "col", LINE_MIDDLE)
    got = [lax.ppermute(give, "col", CORE) for give in (give0, give1, give2)]
    own, near, far = pair_sums([keep0, keep1, keep2], got, 0)
    sums = sums + after(received, own)
    step = 2
    while step < rows:
        sums = exchange_add(sums, "row", rows, step)
        step *= 2
    passed, middle = lax.optimization_barrier((passed, middle))
    far = (far.astype(F32) + passed.astype(F32)).astype(BF16)
    from_far = lax.ppermute(far, "col", LINE_SWAP2)
    near, sums = lax.optimization_barrier((near, sums))
    from_near = lax.ppermute(after(near, far), "col", LINE_SWAP1)
    return [own, middle, from_near, from_far], sums


def per_device(
    features,
    weight,
    bias_vector,
    send_rows,
    send_count,
    adjacency,
    source_tile,
    tile_count,
    cotangent,
):
    rows, columns = lax.axis_size("row"), lax.axis_size("col")
    nodes, width = features.shape
    capacity = send_rows.shape[3]
    tiles, source, count = adjacency[0, 0], source_tile[0, 0], tile_count[0, 0]
    pos = jnp.stack([lax.axis_index("row"), lax.axis_index("col")]).astype(jnp.int32)
    piece = with_lists(features, send_rows[0, 0], send_count[0, 0])
    line = columns == 8 and 2 * tiles.shape[0] * TILE * columns * capacity <= RESIDENT

    if line:
        dense, put_early, put_late, blocks = line_exchange(
            piece,
            lambda: densify(tiles, source, count, pos, rows, columns, capacity),
            pos,
            nodes,
            capacity,
            rows,
        )
    else:
        dense = densify_blocks(tiles, source, count, pos, columns, capacity)
        pieces = [piece] + [
            lax.ppermute(piece, "col", xor_pairs(columns, step)) for step in range(1, columns)
        ]
        here = lax.axis_index("col")
        lists = jnp.stack(
            [
                list_row(
                    lax.dynamic_index_in_dim(a, nodes + here, 0, keepdims=False),
                    lax.dynamic_index_in_dim(a, nodes + columns + here, 0, keepdims=False),
                )
                for a in pieces
            ]
        )
        pick, put = selectors(lists, nodes)
        blocks = forward_blocks(dense, pick, [[a[:nodes]] for a in pieces], pos, rows)

    parts = row_exchange(blocks[0], blocks[1:], rows)
    output, agg, grad_pre, back = layer(weight, bias_vector, cotangent, parts)
    backs = row_exchange(back, [back] * (rows - 1), rows)
    scale = 1.0 / math.sqrt(nodes * rows * columns)
    mine, theirs = weight_partials(agg, grad_pre, pos, scale)
    sums = mine + lax.ppermute(theirs, "col", CORE if line else xor_pairs(columns, 1))

    if line:
        terms, sums = line_reduce(
            dense, put_early, put_late, back, backs[1:], pos, sums, rows, columns
        )
    else:
        scattered = backward_blocks(dense, put, backs, pos, (0,))
        terms = [scattered[0]] + [
            lax.ppermute(scattered[step], "col", xor_pairs(columns, step))
            for step in range(1, columns)
        ]
        step = 2
        while step < columns:
            sums = exchange_add(sums, "col", columns, step)
            step *= 2
        step = 1
        while step < rows:
            sums = exchange_add(sums, "row", rows, step)
            step *= 2
    weight_grad, bias_grad = assemble(
        sums, lax.ppermute(sums, "col", xor_pairs(columns, 1)), pos
    )
    terms[-1], weight_grad, bias_grad = lax.optimization_barrier(
        (terms[-1], weight_grad, bias_grad)
    )
    return output, finish([terms]), weight_grad, bias_grad


def solution(mesh):
    in_specs = (
        P(("row", "col"), None),
        P(),
        P(),
        P("row", "col", None, None),
        P("row", "col", None),
        P("row", "col", None, None, None, None),
        P("row", "col", None, None),
        P("row", "col", None),
        P(("row", "col"), None),
    )
    out_specs = (P(("row", "col"), None), P(("row", "col"), None), P(), P())
    return jax.shard_map(
        per_device, mesh=mesh, in_specs=in_specs, out_specs=out_specs, check_vma=False
    )
```

```python
import functools
import math

import jax
import jax.numpy as jnp
from jax import lax
from jax.experimental import pallas as pl
from jax.experimental.pallas import tpu as pltpu
from jax.sharding import PartitionSpec as P

TILE = 128
VMEM_LIMIT = 16 * 1024 * 1024
BIG_LIMIT = 40 * 1024 * 1024
RESIDENT = 16 * 1024 * 1024
BF16 = jnp.bfloat16
F32 = jnp.float32


def full_spec(shape):
    return pl.BlockSpec(shape, lambda *_: (0,) * len(shape))


def params(limit=VMEM_LIMIT):
    return pltpu.CompilerParams(vmem_limit_bytes=limit)


def xor_pairs(size, step):
    return [(i, i ^ step) for i in range(size)]


def z_pairs(pairs):
    return [(2 * a + core, 2 * b + core) for a, b in pairs for core in range(2)]


def densify_kernel(per_piece, per_peer, src_ref, cnt_ref, pos_ref, adj_ref, out_ref, held, sems):
    targets, slots = adj_ref.shape[0], adj_ref.shape[1]
    here = pos_ref[1]
    whole = slots * TILE == out_ref.shape[1]
    copies = [
        pltpu.make_async_copy(adj_ref.at[t], held.at[t], sems.at[t]) for t in range(targets)
    ]
    for copy in copies:
        copy.start()
    for t, copy in enumerate(copies):
        block = ((t // per_peer) ^ pos_ref[0]) * per_peer + t % per_peer
        rows = pl.ds(pl.multiple_of(block * TILE, TILE), TILE)
        if not whole:
            out_ref[rows, :] = jnp.zeros((TILE, out_ref.shape[1]), out_ref.dtype)
        count = cnt_ref[t]
        copy.wait()
        for s in range(slots):
            source = src_ref[t, s]
            slot = (source // per_piece) ^ here
            place = jnp.where((slot == 3) | (slot == 5), slot ^ 6, slot)
            column = pl.multiple_of((place * per_piece + source % per_piece) * TILE, TILE)
            tile = held[t, s]
            out_ref[rows, pl.ds(column, TILE)] = jnp.where(s < count, tile, jnp.zeros_like(tile))


def densify(adjacency, source_tile, tile_count, pos, peers, pieces, capacity):
    targets = adjacency.shape[0]
    width = pieces * capacity
    smem = pl.BlockSpec(memory_space=pltpu.SMEM)
    return pl.pallas_call(
        functools.partial(densify_kernel, capacity // TILE, targets // peers),
        out_shape=jax.ShapeDtypeStruct((targets * TILE, width), BF16),
        in_specs=[smem, smem, smem, pl.BlockSpec(memory_space=pl.ANY)],
        out_specs=pl.BlockSpec(memory_space=pltpu.VMEM),
        scratch_shapes=[
            pltpu.VMEM(adjacency.shape, BF16),
            pltpu.SemaphoreType.DMA((targets,)),
        ],
        compiler_params=params(40 * 1024 * 1024),
        cost_estimate=pl.CostEstimate(
            flops=0, bytes_accessed=4 * targets * TILE * width, transcendentals=0
        ),
        name="densify",
    )(source_tile, tile_count, pos, adjacency)


def densify_blocks_kernel(per_piece, src_ref, cnt_ref, pos_ref, adj_ref, out_ref):
    step = pl.program_id(0)
    tiles, slots = adj_ref.shape[0], adj_ref.shape[1]
    out_ref[...] = jnp.zeros_like(out_ref)
    here = pos_ref[1]
    for t in range(tiles):
        count = cnt_ref[step * tiles + t]
        for s in range(slots):

            @pl.when(s < count)
            def _(t=t, s=s):
                source = src_ref[step * tiles + t, s]
                slot = (source // per_piece) ^ here
                column = pl.multiple_of((slot * per_piece + source % per_piece) * TILE, TILE)
                out_ref[t * TILE : (t + 1) * TILE, pl.ds(column, TILE)] = adj_ref[t, s]


def densify_blocks(adjacency, source_tile, tile_count, pos, pieces, capacity):
    targets, slots = adjacency.shape[0], adjacency.shape[1]
    tiles = 4
    width = pieces * capacity
    return pl.pallas_call(
        functools.partial(densify_blocks_kernel, capacity // TILE),
        out_shape=jax.ShapeDtypeStruct((targets * TILE, width), BF16),
        grid_spec=pltpu.PrefetchScalarGridSpec(
            num_scalar_prefetch=3,
            grid=(targets // tiles,),
            in_specs=[pl.BlockSpec((tiles, slots, TILE, TILE), lambda i, *_: (i, 0, 0, 0))],
            out_specs=pl.BlockSpec((tiles * TILE, width), lambda i, *_: (i, 0)),
        ),
        compiler_params=params(BIG_LIMIT),
        cost_estimate=pl.CostEstimate(
            flops=0, bytes_accessed=2 * targets * TILE * (width + slots * TILE), transcendentals=0
        ),
        name="densify",
    )(source_tile, tile_count, pos, adjacency)


def hits(row, nodes):
    node = lax.broadcasted_iota(jnp.int32, (nodes, row.shape[1]), 0).astype(F32)
    return jnp.where(node == row, 1.0, 0.0).astype(BF16)


def list_row(high, low):
    return high.astype(F32) * 256.0 + low.astype(F32)


def select_kernel(list_ref, pick_ref, put_ref):
    slots, nodes, _ = put_ref.shape
    for slot in range(slots):
        put = hits(list_ref[slot : slot + 1, :], nodes)
        put_ref[slot] = put
        pick_ref[slot] = put.T


def selectors(lists, nodes):
    pieces, capacity = lists.shape
    return pl.pallas_call(
        select_kernel,
        out_shape=(
            jax.ShapeDtypeStruct((pieces, capacity, nodes), BF16),
            jax.ShapeDtypeStruct((pieces, nodes, capacity), BF16),
        ),
        compiler_params=params(BIG_LIMIT),
        cost_estimate=pl.CostEstimate(
            flops=0, bytes_accessed=4 * pieces * capacity * nodes, transcendentals=0
        ),
        name="selectors",
    )(lists)


def gather_rows(sources, here, put_ref, at):
    nodes, capacity = put_ref.shape[1:]
    columns = (sources[0].shape[0] - nodes) // 2
    piece = sources[0][:nodes, :]
    tail = sources[0][nodes:, :].astype(F32)
    for extra in sources[1:]:
        piece = piece + extra[:nodes, :]
        tail = tail + extra[nodes:, :].astype(F32)
    table = list_row(tail[:columns], tail[columns:])
    mine = lax.broadcasted_iota(jnp.int32, table.shape, 0) == here
    put = hits(jnp.sum(jnp.where(mine, table, 0.0), axis=0, keepdims=True), nodes)
    put_ref[at] = put
    rows = lax.dot_general(put, piece, (((0,), (0,)), ((), ())), preferred_element_type=F32)
    return rows.astype(BF16)


def forward_part_kernel(groups, base, peers, last, pos_ref, dense_ref, *rest):
    total = sum(groups)
    sources, rest = rest[:total], rest[total:]
    if last:
        partial_ref, outs, put_ref, gathered = rest[0], rest[1 : 1 + peers], rest[1 + peers], rest[-1]
    else:
        partial_ref, put_ref, gathered = rest
    here = pos_ref[1]
    capacity = put_ref.shape[2]
    at = 0
    for slot, count in enumerate(groups):
        rows = gather_rows(sources[at : at + count], here, put_ref, slot)
        gathered[slot * capacity : (slot + 1) * capacity, :] = rows
        at += count
    columns = slice(base * capacity, (base + len(groups)) * capacity)
    if not last:
        partial_ref[...] = jnp.dot(
            dense_ref[:, columns], gathered[...], preferred_element_type=F32
        )
        return
    block = outs[0].shape[0]
    for peer in range(peers):
        here_rows = slice(peer * block, (peer + 1) * block)
        result = partial_ref[here_rows, :] + jnp.dot(
            dense_ref[here_rows, columns], gathered[...], preferred_element_type=F32
        )
        outs[peer][...] = result.astype(outs[peer].dtype)


def forward_part(dense, groups, base, pos, peers, nodes, capacity, before=None):
    rows = dense.shape[0]
    flat = [array for group in groups for array in group]
    width = flat[0].shape[1]
    last = before is not None
    put = jax.ShapeDtypeStruct((len(groups), nodes, capacity), BF16)
    if last:
        outs = tuple(
            jax.ShapeDtypeStruct((rows // peers, width), F32 if peer == 0 else BF16)
            for peer in range(peers)
        ) + (put,)
        flat = flat + [before]
    else:
        outs = (jax.ShapeDtypeStruct((rows, width), F32), put)
    depth = len(groups) * capacity
    return pl.pallas_call(
        functools.partial(
            forward_part_kernel, tuple(len(group) for group in groups), base, peers, last
        ),
        out_shape=outs,
        in_specs=[pl.BlockSpec(memory_space=pltpu.SMEM)]
        + [pl.BlockSpec(memory_space=pltpu.VMEM)] * (1 + len(flat)),
        scratch_shapes=[pltpu.VMEM((depth, width), BF16)],
        compiler_params=params(),
        cost_estimate=pl.CostEstimate(
            flops=2 * rows * depth * width, bytes_accessed=2 * rows * depth, transcendentals=0
        ),
        name="forward_late" if last else "forward_early",
    )(pos, dense, *flat)


def forward_blocks_kernel(groups, peers, pos_ref, pick_ref, dense_ref, *rest):
    total = sum(groups)
    sources, outs, gathered = rest[:total], rest[total : total + peers], rest[total + peers]
    step = pl.program_id(0)
    capacity = pick_ref.shape[1]

    @pl.when(step == 0)
    def _():
        at = 0
        for slot, count in enumerate(groups):
            piece = sources[at][...]
            for extra in range(1, count):
                piece = piece + sources[at + extra][...]
            at += count
            rows = jnp.dot(pick_ref[slot], piece, preferred_element_type=F32)
            gathered[slot * capacity : (slot + 1) * capacity, :] = rows.astype(BF16)

    result = jnp.dot(dense_ref[...], gathered[...], preferred_element_type=F32)
    for peer in range(peers):

        @pl.when(step == peer)
        def _(peer=peer):
            outs[peer][...] = result.astype(outs[peer].dtype)


def forward_blocks(dense, pick, groups, pos, peers):
    rows, width = dense.shape
    flat = [array for group in groups for array in group]
    nodes, chunk = flat[0].shape
    block = rows // peers
    return pl.pallas_call(
        functools.partial(forward_blocks_kernel, tuple(len(group) for group in groups), peers),
        out_shape=tuple(
            jax.ShapeDtypeStruct((block, chunk), F32 if peer == 0 else BF16)
            for peer in range(peers)
        ),
        grid_spec=pltpu.PrefetchScalarGridSpec(
            num_scalar_prefetch=1,
            grid=(peers,),
            in_specs=[
                full_spec(pick.shape),
                pl.BlockSpec((block, width), lambda i, pos_ref: (i ^ pos_ref[0], 0)),
            ]
            + [full_spec((nodes, chunk))] * len(flat),
            out_specs=tuple(full_spec((block, chunk)) for _ in range(peers)),
            scratch_shapes=[pltpu.VMEM((width, chunk), BF16)],
        ),
        compiler_params=params(BIG_LIMIT),
        cost_estimate=pl.CostEstimate(
            flops=2 * rows * width * chunk, bytes_accessed=2 * rows * width, transcendentals=0
        ),
        name="forward_rows",
    )(pos, pick, dense, *flat)


def layer_kernel(peers, weight_ref, bias_ref, cot_ref, *rest):
    parts, outs = rest[:peers], rest[peers:]
    out_ref, agg_ref, grad_ref = outs[:3]
    total = parts[0][...].astype(F32)
    for peer in range(1, peers):
        total = total + parts[peer][...].astype(F32)
    agg = total.astype(BF16)
    weight = weight_ref[...]
    preact = jnp.dot(agg, weight, preferred_element_type=F32) + bias_ref[...]
    sigma = 1.0 / (1.0 + jnp.exp(-preact))
    out_ref[...] = (preact * sigma).astype(BF16)
    grad = (cot_ref[...].astype(F32) * sigma * (1.0 + preact * (1.0 - sigma))).astype(BF16)
    agg_ref[...] = agg
    grad_ref[...] = grad
    outs[3][...] = lax.dot_general(
        grad, weight, (((1,), (1,)), ((), ())), preferred_element_type=F32
    ).astype(BF16)


def layer(weight, bias_vector, cotangent, parts):
    nodes, width = cotangent.shape
    return pl.pallas_call(
        functools.partial(layer_kernel, len(parts)),
        out_shape=(jax.ShapeDtypeStruct((nodes, width), BF16),) * 4,
        compiler_params=params(),
        cost_estimate=pl.CostEstimate(
            flops=4 * nodes * width * width,
            bytes_accessed=2 * nodes * width * 10,
            transcendentals=nodes * width,
        ),
        name="layer",
    )(weight, bias_vector.reshape(1, -1), cotangent, *parts)


def weights_kernel(scale, pos_ref, agg_ref, grad_ref, mine_ref, theirs_ref):
    grad = grad_ref[...]
    product = scale * lax.dot_general(
        agg_ref[...], grad, (((0,), (0,)), ((), ())), preferred_element_type=F32
    )
    bias = scale * jnp.sum(grad.astype(F32).reshape(-1, 8, grad.shape[1]), axis=0)
    half = product.shape[0] // 2
    core = pos_ref[1] % 2
    for keep, give, parity in ((mine_ref, theirs_ref, 0), (theirs_ref, mine_ref, 1)):

        @pl.when(core == parity)
        def _(keep=keep, give=give):
            keep[:half] = product[:half]
            give[:half] = product[half:]

    mine_ref[half:] = bias
    theirs_ref[half:] = bias


def weight_partials(agg, grad, pos, scale):
    nodes, width = agg.shape
    return pl.pallas_call(
        functools.partial(weights_kernel, scale),
        out_shape=(jax.ShapeDtypeStruct((width // 2 + 8, width), F32),) * 2,
        in_specs=[pl.BlockSpec(memory_space=pltpu.SMEM)]
        + [pl.BlockSpec(memory_space=pltpu.VMEM)] * 2,
        compiler_params=params(),
        cost_estimate=pl.CostEstimate(
            flops=2 * nodes * width * width, bytes_accessed=6 * nodes * width, transcendentals=0
        ),
        name="weight_partials",
    )(pos, agg, grad)


def assemble_kernel(pos_ref, mine_ref, theirs_ref, weight_ref, bias_ref):
    half = weight_ref.shape[0] // 2
    core = pos_ref[1] % 2
    mine = pl.multiple_of(core * half, half)
    theirs = pl.multiple_of((1 - core) * half, half)
    weight_ref[pl.ds(mine, half), :] = mine_ref[:half]
    weight_ref[pl.ds(theirs, half), :] = theirs_ref[:half]
    bias_ref[...] = jnp.sum(mine_ref[half:], axis=0, keepdims=True)


def assemble(mine, theirs, pos):
    width = mine.shape[1]
    weight, bias = pl.pallas_call(
        assemble_kernel,
        out_shape=(
            jax.ShapeDtypeStruct((width, width), F32),
            jax.ShapeDtypeStruct((1, width), F32),
        ),
        in_specs=[pl.BlockSpec(memory_space=pltpu.SMEM)]
        + [pl.BlockSpec(memory_space=pltpu.VMEM)] * 2,
        compiler_params=params(),
        cost_estimate=pl.CostEstimate(
            flops=0, bytes_accessed=16 * width * width, transcendentals=0
        ),
        name="assemble",
    )(pos, mine, theirs)
    return weight, bias.reshape(width)


def back_product(dense, back):
    return lax.dot_general(
        dense, back, (((0,), (0,)), ((), ())), preferred_element_type=F32
    )


def backward_early_kernel(dense_ref, back_ref, out_ref):
    out_ref[...] = back_product(dense_ref[: back_ref.shape[0], :], back_ref[...])


def backward_early(dense, back):
    width, size = dense.shape[1], back.shape[1]
    return pl.pallas_call(
        backward_early_kernel,
        out_shape=jax.ShapeDtypeStruct((width, size), F32),
        compiler_params=params(),
        cost_estimate=pl.CostEstimate(
            flops=2 * width * back.size, bytes_accessed=6 * width * size, transcendentals=0
        ),
        name="backward_early",
    )(dense, back)


def backward_late_kernel(base, slots, peers, dense_ref, *rest):
    puts, rest = rest[: len(slots)], rest[len(slots) :]
    first_ref, rest = rest[0], rest[1:]
    backs, outs, (joined, rows) = rest[: peers - 1], rest[peers - 1 : -2], rest[-2:]
    capacity = puts[0].shape[2]
    block = backs[0].shape[0]
    for peer in range(1, peers):
        joined[(peer - 1) * block : peer * block, :] = backs[peer - 1][...]
    columns = slice(base * capacity, (base + len(outs)) * capacity)
    rows[...] = (
        first_ref[columns, :] + back_product(dense_ref[block:, columns], joined[...])
    ).astype(BF16)
    at = 0
    for put_ref, picked in zip(puts, slots):
        for slot in picked:
            outs[at][...] = jnp.dot(
                put_ref[slot],
                rows[at * capacity : (at + 1) * capacity, :],
                preferred_element_type=F32,
            ).astype(outs[at].dtype)
            at += 1


def backward_late(dense, puts, slots, first, backs, base):
    _, nodes, capacity = puts[0].shape
    count = sum(len(picked) for picked in slots)
    size = first.shape[1]
    return pl.pallas_call(
        functools.partial(backward_late_kernel, base, slots, len(backs) + 1),
        out_shape=tuple(
            jax.ShapeDtypeStruct((nodes, size), BF16 if (base + at) % 2 else F32)
            for at in range(count)
        ),
        scratch_shapes=[
            pltpu.VMEM((len(backs) * backs[0].shape[0], size), BF16),
            pltpu.VMEM((count * capacity, size), BF16),
        ],
        compiler_params=params(),
        cost_estimate=pl.CostEstimate(
            flops=2 * count * capacity * size * dense.shape[0],
            bytes_accessed=2 * dense.shape[0] * count * capacity,
            transcendentals=0,
        ),
        name="backward_late",
    )(dense, *puts, first, *backs)


def backward_blocks_kernel(peers, slots, pos_ref, put_ref, dense_ref, *rest):
    backs, outs, total = rest[:peers], rest[peers : peers + slots], rest[peers + slots]
    step = pl.program_id(0)
    capacity = put_ref.shape[2]
    for peer in range(peers):

        @pl.when(step == peer)
        def _(peer=peer):
            product = lax.dot_general(
                dense_ref[...], backs[peer][...], (((0,), (0,)), ((), ())), preferred_element_type=F32
            )
            if peer == 0:
                total[...] = product
            else:
                total[...] += product

    @pl.when(step == peers - 1)
    def _():
        for slot in range(slots):
            rows = total[slot * capacity : (slot + 1) * capacity, :].astype(BF16)
            outs[slot][...] = jnp.dot(put_ref[slot], rows, preferred_element_type=F32).astype(
                outs[slot].dtype
            )


def backward_blocks(dense, put, backs, pos, kept):
    peers = len(backs)
    rows, width = dense.shape
    slots, nodes, _ = put.shape
    chunk = backs[0].shape[1]
    block = rows // peers
    return pl.pallas_call(
        functools.partial(backward_blocks_kernel, peers, slots),
        out_shape=tuple(
            jax.ShapeDtypeStruct((nodes, chunk), F32 if slot in kept else BF16)
            for slot in range(slots)
        ),
        grid_spec=pltpu.PrefetchScalarGridSpec(
            num_scalar_prefetch=1,
            grid=(peers,),
            in_specs=[
                full_spec(put.shape),
                pl.BlockSpec((block, width), lambda i, pos_ref: (i ^ pos_ref[0], 0)),
            ]
            + [full_spec((block, chunk))] * peers,
            out_specs=tuple(full_spec((nodes, chunk)) for _ in range(slots)),
            scratch_shapes=[pltpu.VMEM((width, chunk), F32)],
        ),
        compiler_params=params(BIG_LIMIT),
        cost_estimate=pl.CostEstimate(
            flops=2 * rows * width * chunk, bytes_accessed=2 * rows * width, transcendentals=0
        ),
        name="backward_rows",
    )(pos, put, dense, *backs)


def pair_sum_kernel(count, *refs):
    for i in range(count):
        total = refs[i][...].astype(F32) + refs[count + i][...].astype(F32)
        refs[2 * count + i][...] = total.astype(refs[2 * count + i].dtype)


def pair_sums(kept, received, wide=-1):
    count = len(kept)
    return pl.pallas_call(
        functools.partial(pair_sum_kernel, count),
        out_shape=tuple(
            jax.ShapeDtypeStruct(kept[i].shape, F32 if i == wide else BF16) for i in range(count)
        ),
        compiler_params=params(),
        cost_estimate=pl.CostEstimate(
            flops=0, bytes_accessed=count * kept[0].size * 8, transcendentals=0
        ),
        name="pair_sums",
    )(*kept, *received)


def finish_kernel(chunks, each, *refs):
    out_ref = refs[-1]
    size = out_ref.shape[1] // chunks
    for chunk in range(chunks):
        total = refs[chunk * each][...].astype(F32)
        for term in range(1, each):
            total = total + refs[chunk * each + term][...].astype(F32)
        out_ref[:, chunk * size : (chunk + 1) * size] = total.astype(BF16)


def finish(terms):
    chunks, each = len(terms), len(terms[0])
    nodes, size = terms[0][0].shape
    return pl.pallas_call(
        functools.partial(finish_kernel, chunks, each),
        out_shape=jax.ShapeDtypeStruct((nodes, size * chunks), BF16),
        compiler_params=params(),
        cost_estimate=pl.CostEstimate(
            flops=0, bytes_accessed=chunks * nodes * size * 2 * each, transcendentals=0
        ),
        name="finish",
    )(*[array for group in terms for array in group])


LINE_SWAP1 = z_pairs([(0, 1), (1, 0), (2, 3), (3, 2)])
LINE_SWAP2 = z_pairs([(0, 2), (2, 0), (1, 3), (3, 1)])
LINE_MIDDLE = z_pairs([(1, 2), (2, 1)])
LINE_OUT = z_pairs([(2, 3), (1, 0)])
LINE_IN = z_pairs([(3, 2), (0, 1)])
CORE = xor_pairs(8, 1)


def after(value, *others):
    return lax.optimization_barrier((value,) + others)[0]


def exchange_add(value, axis, size, step):
    return value + lax.ppermute(value, axis, xor_pairs(size, step))


def with_lists(features, list_rows, list_counts):
    live = jnp.arange(list_rows.shape[1])[None, :] < list_counts[:, None]
    high = jnp.where(live, list_rows // 256, -1)
    low = jnp.where(live, list_rows % 256, 0)
    return jnp.concatenate([features, high.astype(BF16), low.astype(BF16)], axis=0)


def line_exchange(piece, dense_of, pos, nodes, capacity, rows):
    far = lax.ppermute(piece, "col", LINE_SWAP2)
    near = lax.ppermute(piece, "col", LINE_SWAP1)
    other = lax.ppermute(piece, "col", CORE)
    dense = dense_of()
    far, dense = lax.optimization_barrier((far, dense))
    ends = lax.ppermute(far, "col", LINE_OUT)
    middle = lax.ppermute(after(piece, far), "col", LINE_MIDDLE)
    early = [[piece], [other], [near], [lax.ppermute(far, "col", CORE)], [far]]
    partial, put_early = forward_part(dense, early, 0, pos, rows, nodes, capacity)
    partial, middle, ends = lax.optimization_barrier((partial, middle, ends))
    late = [
        [lax.ppermute(near, "col", CORE)],
        [middle, ends],
        [lax.ppermute(middle, "col", CORE), lax.ppermute(ends, "col", CORE)],
    ]
    *blocks, put_late = forward_part(dense, late, 5, pos, rows, nodes, capacity, partial)
    return dense, put_early, put_late, blocks


def row_exchange(own, arrays, rows):
    received = [
        lax.ppermute(arrays[step - 1], "row", xor_pairs(rows, step))
        for step in reversed(range(1, rows))
    ]
    return [own] + received[::-1]


def line_reduce(dense, put_early, put_late, back, backs, pos, sums, rows, columns):
    first = backward_early(dense, back)
    sums = sums + after(lax.ppermute(sums, "col", xor_pairs(columns, 2)), backs[2])
    sums = exchange_add(sums, "col", columns, 4)
    *backs, first, sums = lax.optimization_barrier((*backs, first, sums))
    keep3, give3 = backward_late(dense, (put_late,), ((1, 2),), first, backs, 6)
    got3 = lax.ppermute(give3, "col", CORE)
    received = lax.ppermute(sums, "row", xor_pairs(rows, 1))
    keep0, give0, keep1, give2, keep2, give1 = backward_late(
        dense, (put_early, put_late), (tuple(range(5)), (0,)), first, backs, 0
    )
    got3, give2, give1, give0, keep0 = lax.optimization_barrier((got3, give2, give1, give0, keep0))
    (last,) = pair_sums([keep3], [got3])
    passed = lax.ppermute(last, "col", LINE_IN)
    middle = lax.ppermute(last, "col", LINE_MIDDLE)
    got = [lax.ppermute(give, "col", CORE) for give in (give0, give1, give2)]
    own, near, far = pair_sums([keep0, keep1, keep2], got, 0)
    sums = sums + after(received, own)
    step = 2
    while step < rows:
        sums = exchange_add(sums, "row", rows, step)
        step *= 2
    passed, middle = lax.optimization_barrier((passed, middle))
    far = (far.astype(F32) + passed.astype(F32)).astype(BF16)
    from_far = lax.ppermute(far, "col", LINE_SWAP2)
    near, sums = lax.optimization_barrier((near, sums))
    from_near = lax.ppermute(after(near, far), "col", LINE_SWAP1)
    return [own, middle, from_near, from_far], sums


def per_device(
    features,
    weight,
    bias_vector,
    send_rows,
    send_count,
    adjacency,
    source_tile,
    tile_count,
    cotangent,
):
    rows, columns = lax.axis_size("row"), lax.axis_size("col")
    nodes, width = features.shape
    capacity = send_rows.shape[3]
    tiles, source, count = adjacency[0, 0], source_tile[0, 0], tile_count[0, 0]
    pos = jnp.stack([lax.axis_index("row"), lax.axis_index("col")]).astype(jnp.int32)
    piece = with_lists(features, send_rows[0, 0], send_count[0, 0])
    line = columns == 8 and 2 * tiles.shape[0] * TILE * columns * capacity <= RESIDENT

    if line:
        dense, put_early, put_late, blocks = line_exchange(
            piece,
            lambda: densify(tiles, source, count, pos, rows, columns, capacity),
            pos,
            nodes,
            capacity,
            rows,
        )
    else:
        dense = densify_blocks(tiles, source, count, pos, columns, capacity)
        pieces = [piece] + [
            lax.ppermute(piece, "col", xor_pairs(columns, step)) for step in range(1, columns)
        ]
        here = lax.axis_index("col")
        lists = jnp.stack(
            [
                list_row(
                    lax.dynamic_index_in_dim(a, nodes + here, 0, keepdims=False),
                    lax.dynamic_index_in_dim(a, nodes + columns + here, 0, keepdims=False),
                )
                for a in pieces
            ]
        )
        pick, put = selectors(lists, nodes)
        blocks = forward_blocks(dense, pick, [[a[:nodes]] for a in pieces], pos, rows)

    parts = row_exchange(blocks[0], blocks[1:], rows)
    output, agg, grad_pre, back = layer(weight, bias_vector, cotangent, parts)
    backs = row_exchange(back, [back] * (rows - 1), rows)
    scale = 1.0 / math.sqrt(nodes * rows * columns)
    mine, theirs = weight_partials(agg, grad_pre, pos, scale)
    sums = mine + lax.ppermute(theirs, "col", CORE if line else xor_pairs(columns, 1))

    if line:
        terms, sums = line_reduce(
            dense, put_early, put_late, back, backs[1:], pos, sums, rows, columns
        )
    else:
        scattered = backward_blocks(dense, put, backs, pos, (0,))
        terms = [scattered[0]] + [
            lax.ppermute(scattered[step], "col", xor_pairs(columns, step))
            for step in range(1, columns)
        ]
        step = 2
        while step < columns:
            sums = exchange_add(sums, "col", columns, step)
            step *= 2
        step = 1
        while step < rows:
            sums = exchange_add(sums, "row", rows, step)
            step *= 2
    weight_grad, bias_grad = assemble(
        sums, lax.ppermute(sums, "col", xor_pairs(columns, 1)), pos
    )
    terms[-1], weight_grad, bias_grad = lax.optimization_barrier(
        (terms[-1], weight_grad, bias_grad)
    )
    return output, finish([terms]), weight_grad, bias_grad


def solution(mesh):
    in_specs = (
        P(("row", "col"), None),
        P(),
        P(),
        P("row", "col", None, None),
        P("row", "col", None),
        P("row", "col", None, None, None, None),
        P("row", "col", None, None),
        P("row", "col", None),
        P(("row", "col"), None),
    )
    out_specs = (P(("row", "col"), None), P(("row", "col"), None), P(), P())
    return jax.shard_map(
        per_device, mesh=mesh, in_specs=in_specs, out_specs=out_specs, check_vma=False
    )
```

```python
import functools
import math

import jax
import jax.numpy as jnp
from jax import lax
from jax.experimental import pallas as pl
from jax.experimental.pallas import tpu as pltpu
from jax.sharding import PartitionSpec as P

TILE = 128
VMEM_LIMIT = 16 * 1024 * 1024
BIG_LIMIT = 40 * 1024 * 1024
RESIDENT = 16 * 1024 * 1024
BF16 = jnp.bfloat16
F32 = jnp.float32


def full_spec(shape):
    return pl.BlockSpec(shape, lambda *_: (0,) * len(shape))


def params(limit=VMEM_LIMIT):
    return pltpu.CompilerParams(vmem_limit_bytes=limit)


def xor_pairs(size, step):
    return [(i, i ^ step) for i in range(size)]


def z_pairs(pairs):
    return [(2 * a + core, 2 * b + core) for a, b in pairs for core in range(2)]


def densify_kernel(per_piece, per_peer, src_ref, cnt_ref, pos_ref, adj_ref, out_ref, held, sems):
    targets, slots = adj_ref.shape[0], adj_ref.shape[1]
    here = pos_ref[1]
    whole = slots * TILE == out_ref.shape[1]
    copies = [
        pltpu.make_async_copy(adj_ref.at[t], held.at[t], sems.at[t]) for t in range(targets)
    ]
    for copy in copies:
        copy.start()
    for t, copy in enumerate(copies):
        block = ((t // per_peer) ^ pos_ref[0]) * per_peer + t % per_peer
        rows = pl.ds(pl.multiple_of(block * TILE, TILE), TILE)
        if not whole:
            out_ref[rows, :] = jnp.zeros((TILE, out_ref.shape[1]), out_ref.dtype)
        count = cnt_ref[t]
        copy.wait()
        for s in range(slots):
            source = src_ref[t, s]
            slot = (source // per_piece) ^ here
            place = jnp.where((slot == 3) | (slot == 5), slot ^ 6, slot)
            column = pl.multiple_of((place * per_piece + source % per_piece) * TILE, TILE)
            tile = held[t, s]
            out_ref[rows, pl.ds(column, TILE)] = jnp.where(s < count, tile, jnp.zeros_like(tile))


def densify(adjacency, source_tile, tile_count, pos, peers, pieces, capacity):
    targets = adjacency.shape[0]
    width = pieces * capacity
    smem = pl.BlockSpec(memory_space=pltpu.SMEM)
    return pl.pallas_call(
        functools.partial(densify_kernel, capacity // TILE, targets // peers),
        out_shape=jax.ShapeDtypeStruct((targets * TILE, width), BF16),
        in_specs=[smem, smem, smem, pl.BlockSpec(memory_space=pl.ANY)],
        out_specs=pl.BlockSpec(memory_space=pltpu.VMEM),
        scratch_shapes=[
            pltpu.VMEM(adjacency.shape, BF16),
            pltpu.SemaphoreType.DMA((targets,)),
        ],
        compiler_params=params(40 * 1024 * 1024),
        cost_estimate=pl.CostEstimate(
            flops=0, bytes_accessed=4 * targets * TILE * width, transcendentals=0
        ),
        name="densify",
    )(source_tile, tile_count, pos, adjacency)


def densify_blocks_kernel(per_piece, src_ref, cnt_ref, pos_ref, adj_ref, out_ref):
    step = pl.program_id(0)
    tiles, slots = adj_ref.shape[0], adj_ref.shape[1]
    out_ref[...] = jnp.zeros_like(out_ref)
    here = pos_ref[1]
    for t in range(tiles):
        count = cnt_ref[step * tiles + t]
        for s in range(slots):

            @pl.when(s < count)
            def _(t=t, s=s):
                source = src_ref[step * tiles + t, s]
                slot = (source // per_piece) ^ here
                column = pl.multiple_of((slot * per_piece + source % per_piece) * TILE, TILE)
                out_ref[t * TILE : (t + 1) * TILE, pl.ds(column, TILE)] = adj_ref[t, s]


def densify_blocks(adjacency, source_tile, tile_count, pos, pieces, capacity):
    targets, slots = adjacency.shape[0], adjacency.shape[1]
    tiles = 4
    width = pieces * capacity
    return pl.pallas_call(
        functools.partial(densify_blocks_kernel, capacity // TILE),
        out_shape=jax.ShapeDtypeStruct((targets * TILE, width), BF16),
        grid_spec=pltpu.PrefetchScalarGridSpec(
            num_scalar_prefetch=3,
            grid=(targets // tiles,),
            in_specs=[pl.BlockSpec((tiles, slots, TILE, TILE), lambda i, *_: (i, 0, 0, 0))],
            out_specs=pl.BlockSpec((tiles * TILE, width), lambda i, *_: (i, 0)),
        ),
        compiler_params=params(BIG_LIMIT),
        cost_estimate=pl.CostEstimate(
            flops=0, bytes_accessed=2 * targets * TILE * (width + slots * TILE), transcendentals=0
        ),
        name="densify",
    )(source_tile, tile_count, pos, adjacency)


def hits(row, nodes):
    node = lax.broadcasted_iota(jnp.int32, (nodes, row.shape[1]), 0).astype(F32)
    return jnp.where(node == row, 1.0, 0.0).astype(BF16)


def list_row(high, low):
    return high.astype(F32) * 256.0 + low.astype(F32)


def select_kernel(list_ref, pick_ref, put_ref):
    slots, nodes, _ = put_ref.shape
    for slot in range(slots):
        put = hits(list_ref[slot : slot + 1, :], nodes)
        put_ref[slot] = put
        pick_ref[slot] = put.T


def selectors(lists, nodes):
    pieces, capacity = lists.shape
    return pl.pallas_call(
        select_kernel,
        out_shape=(
            jax.ShapeDtypeStruct((pieces, capacity, nodes), BF16),
            jax.ShapeDtypeStruct((pieces, nodes, capacity), BF16),
        ),
        compiler_params=params(BIG_LIMIT),
        cost_estimate=pl.CostEstimate(
            flops=0, bytes_accessed=4 * pieces * capacity * nodes, transcendentals=0
        ),
        name="selectors",
    )(lists)


def gather_rows(sources, here, put_ref, at):
    nodes, capacity = put_ref.shape[1:]
    columns = (sources[0].shape[0] - nodes) // 2
    piece = sources[0][:nodes, :]
    tail = sources[0][nodes:, :].astype(F32)
    for extra in sources[1:]:
        piece = piece + extra[:nodes, :]
        tail = tail + extra[nodes:, :].astype(F32)
    table = list_row(tail[:columns], tail[columns:])
    mine = lax.broadcasted_iota(jnp.int32, table.shape, 0) == here
    put = hits(jnp.sum(jnp.where(mine, table, 0.0), axis=0, keepdims=True), nodes)
    put_ref[at] = put
    rows = lax.dot_general(put, piece, (((0,), (0,)), ((), ())), preferred_element_type=F32)
    return rows.astype(BF16)


def forward_part_kernel(groups, base, peers, added, last, pos_ref, dense_ref, *rest):
    total = sum(groups)
    sources, rest = rest[:total], list(rest[total:])
    before_ref = rest.pop(0) if added else None
    *outs, put_ref, gathered = rest
    here = pos_ref[1]
    capacity = put_ref.shape[2]
    at = 0
    for slot, count in enumerate(groups):
        rows = gather_rows(sources[at : at + count], here, put_ref, slot)
        gathered[slot * capacity : (slot + 1) * capacity, :] = rows
        at += count
    columns = slice(base * capacity, (base + len(groups)) * capacity)
    block = dense_ref.shape[0] // peers
    for peer in range(peers):
        here_rows = slice(peer * block, (peer + 1) * block)
        result = jnp.dot(
            dense_ref[here_rows, columns], gathered[...], preferred_element_type=F32
        )
        if added:
            result = before_ref[here_rows, :] + result
        if last:
            outs[peer][...] = result.astype(outs[peer].dtype)
        else:
            outs[0][here_rows, :] = result


def forward_part(dense, groups, base, pos, peers, nodes, capacity, before=None, last=False):
    rows = dense.shape[0]
    flat = [array for group in groups for array in group]
    width = flat[0].shape[1]
    added = before is not None
    if last:
        outs = tuple(
            jax.ShapeDtypeStruct((rows // peers, width), F32 if peer == 0 else BF16)
            for peer in range(peers)
        )
    else:
        outs = (jax.ShapeDtypeStruct((rows, width), F32),)
    depth = len(groups) * capacity
    if added:
        flat = flat + [before]
    return pl.pallas_call(
        functools.partial(
            forward_part_kernel, tuple(len(group) for group in groups), base, peers, added, last
        ),
        out_shape=outs + (jax.ShapeDtypeStruct((len(groups), nodes, capacity), BF16),),
        in_specs=[pl.BlockSpec(memory_space=pltpu.SMEM)]
        + [pl.BlockSpec(memory_space=pltpu.VMEM)] * (1 + len(flat)),
        scratch_shapes=[pltpu.VMEM((depth, width), BF16)],
        compiler_params=params(),
        cost_estimate=pl.CostEstimate(
            flops=2 * rows * depth * width, bytes_accessed=2 * rows * depth, transcendentals=0
        ),
        name="forward_last" if last else "forward_part",
    )(pos, dense, *flat)


def forward_blocks_kernel(groups, peers, pos_ref, pick_ref, dense_ref, *rest):
    total = sum(groups)
    sources, outs, gathered = rest[:total], rest[total : total + peers], rest[total + peers]
    step = pl.program_id(0)
    capacity = pick_ref.shape[1]

    @pl.when(step == 0)
    def _():
        at = 0
        for slot, count in enumerate(groups):
            piece = sources[at][...]
            for extra in range(1, count):
                piece = piece + sources[at + extra][...]
            at += count
            rows = jnp.dot(pick_ref[slot], piece, preferred_element_type=F32)
            gathered[slot * capacity : (slot + 1) * capacity, :] = rows.astype(BF16)

    result = jnp.dot(dense_ref[...], gathered[...], preferred_element_type=F32)
    for peer in range(peers):

        @pl.when(step == peer)
        def _(peer=peer):
            outs[peer][...] = result.astype(outs[peer].dtype)


def forward_blocks(dense, pick, groups, pos, peers):
    rows, width = dense.shape
    flat = [array for group in groups for array in group]
    nodes, chunk = flat[0].shape
    block = rows // peers
    return pl.pallas_call(
        functools.partial(forward_blocks_kernel, tuple(len(group) for group in groups), peers),
        out_shape=tuple(
            jax.ShapeDtypeStruct((block, chunk), F32 if peer == 0 else BF16)
            for peer in range(peers)
        ),
        grid_spec=pltpu.PrefetchScalarGridSpec(
            num_scalar_prefetch=1,
            grid=(peers,),
            in_specs=[
                full_spec(pick.shape),
                pl.BlockSpec((block, width), lambda i, pos_ref: (i ^ pos_ref[0], 0)),
            ]
            + [full_spec((nodes, chunk))] * len(flat),
            out_specs=tuple(full_spec((block, chunk)) for _ in range(peers)),
            scratch_shapes=[pltpu.VMEM((width, chunk), BF16)],
        ),
        compiler_params=params(BIG_LIMIT),
        cost_estimate=pl.CostEstimate(
            flops=2 * rows * width * chunk, bytes_accessed=2 * rows * width, transcendentals=0
        ),
        name="forward_rows",
    )(pos, pick, dense, *flat)


def layer_kernel(peers, scale, pos_ref, weight_ref, bias_ref, cot_ref, *rest):
    parts, (out_ref, back_ref, mine_ref, theirs_ref) = rest[:peers], rest[peers:]
    total = parts[0][...].astype(F32)
    for peer in range(1, peers):
        total = total + parts[peer][...].astype(F32)
    agg = total.astype(BF16)
    weight = weight_ref[...]
    preact = jnp.dot(agg, weight, preferred_element_type=F32) + bias_ref[...]
    sigma = 1.0 / (1.0 + jnp.exp(-preact))
    out_ref[...] = (preact * sigma).astype(BF16)
    grad = (cot_ref[...].astype(F32) * sigma * (1.0 + preact * (1.0 - sigma))).astype(BF16)
    back_ref[...] = lax.dot_general(
        grad, weight, (((1,), (1,)), ((), ())), preferred_element_type=F32
    ).astype(BF16)
    product = scale * lax.dot_general(
        agg, grad, (((0,), (0,)), ((), ())), preferred_element_type=F32
    )
    bias = scale * jnp.sum(grad.astype(F32).reshape(-1, 8, grad.shape[1]), axis=0)
    half = product.shape[0] // 2
    core = pos_ref[1] % 2
    for keep, give, parity in ((mine_ref, theirs_ref, 0), (theirs_ref, mine_ref, 1)):

        @pl.when(core == parity)
        def _(keep=keep, give=give):
            keep[:half] = product[:half]
            give[:half] = product[half:]

    mine_ref[half:] = bias
    theirs_ref[half:] = bias


def layer(weight, bias_vector, cotangent, parts, pos, scale):
    nodes, width = cotangent.shape
    return pl.pallas_call(
        functools.partial(layer_kernel, len(parts), scale),
        out_shape=(jax.ShapeDtypeStruct((nodes, width), BF16),) * 2
        + (jax.ShapeDtypeStruct((width // 2 + 8, width), F32),) * 2,
        in_specs=[pl.BlockSpec(memory_space=pltpu.SMEM)]
        + [pl.BlockSpec(memory_space=pltpu.VMEM)] * (3 + len(parts)),
        compiler_params=params(),
        cost_estimate=pl.CostEstimate(
            flops=6 * nodes * width * width,
            bytes_accessed=2 * nodes * width * 10,
            transcendentals=nodes * width,
        ),
        name="layer",
    )(pos, weight, bias_vector.reshape(1, -1), cotangent, *parts)


def assemble_kernel(pos_ref, mine_ref, theirs_ref, weight_ref, bias_ref):
    half = weight_ref.shape[0] // 2
    core = pos_ref[1] % 2
    mine = pl.multiple_of(core * half, half)
    theirs = pl.multiple_of((1 - core) * half, half)
    weight_ref[pl.ds(mine, half), :] = mine_ref[:half]
    weight_ref[pl.ds(theirs, half), :] = theirs_ref[:half]
    bias_ref[...] = jnp.sum(mine_ref[half:], axis=0, keepdims=True)


def assemble(mine, theirs, pos):
    width = mine.shape[1]
    weight, bias = pl.pallas_call(
        assemble_kernel,
        out_shape=(
            jax.ShapeDtypeStruct((width, width), F32),
            jax.ShapeDtypeStruct((1, width), F32),
        ),
        in_specs=[pl.BlockSpec(memory_space=pltpu.SMEM)]
        + [pl.BlockSpec(memory_space=pltpu.VMEM)] * 2,
        compiler_params=params(),
        cost_estimate=pl.CostEstimate(
            flops=0, bytes_accessed=16 * width * width, transcendentals=0
        ),
        name="assemble",
    )(pos, mine, theirs)
    return weight, bias.reshape(width)


def back_product(dense, back):
    return lax.dot_general(
        dense, back, (((0,), (0,)), ((), ())), preferred_element_type=F32
    )


def backward_early_kernel(dense_ref, back_ref, out_ref):
    out_ref[...] = back_product(dense_ref[: back_ref.shape[0], :], back_ref[...])


def backward_early(dense, back):
    width, size = dense.shape[1], back.shape[1]
    return pl.pallas_call(
        backward_early_kernel,
        out_shape=jax.ShapeDtypeStruct((width, size), F32),
        compiler_params=params(),
        cost_estimate=pl.CostEstimate(
            flops=2 * width * back.size, bytes_accessed=6 * width * size, transcendentals=0
        ),
        name="backward_early",
    )(dense, back)


def backward_late_kernel(base, slots, peers, dense_ref, *rest):
    puts, rest = rest[: len(slots)], rest[len(slots) :]
    first_ref, rest = rest[0], rest[1:]
    backs, outs, (joined, rows) = rest[: peers - 1], rest[peers - 1 : -2], rest[-2:]
    capacity = puts[0].shape[2]
    block = backs[0].shape[0]
    for peer in range(1, peers):
        joined[(peer - 1) * block : peer * block, :] = backs[peer - 1][...]
    columns = slice(base * capacity, (base + len(outs)) * capacity)
    rows[...] = (
        first_ref[columns, :] + back_product(dense_ref[block:, columns], joined[...])
    ).astype(BF16)
    at = 0
    for put_ref, picked in zip(puts, slots):
        for slot in picked:
            outs[at][...] = jnp.dot(
                put_ref[slot],
                rows[at * capacity : (at + 1) * capacity, :],
                preferred_element_type=F32,
            ).astype(outs[at].dtype)
            at += 1


def backward_late(dense, puts, slots, first, backs, base):
    _, nodes, capacity = puts[0].shape
    count = sum(len(picked) for picked in slots)
    size = first.shape[1]
    return pl.pallas_call(
        functools.partial(backward_late_kernel, base, slots, len(backs) + 1),
        out_shape=tuple(
            jax.ShapeDtypeStruct((nodes, size), BF16 if (base + at) % 2 else F32)
            for at in range(count)
        ),
        scratch_shapes=[
            pltpu.VMEM((len(backs) * backs[0].shape[0], size), BF16),
            pltpu.VMEM((count * capacity, size), BF16),
        ],
        compiler_params=params(),
        cost_estimate=pl.CostEstimate(
            flops=2 * count * capacity * size * dense.shape[0],
            bytes_accessed=2 * dense.shape[0] * count * capacity,
            transcendentals=0,
        ),
        name="backward_late",
    )(dense, *puts, first, *backs)


def backward_blocks_kernel(peers, slots, pos_ref, put_ref, dense_ref, *rest):
    backs, outs, total = rest[:peers], rest[peers : peers + slots], rest[peers + slots]
    step = pl.program_id(0)
    capacity = put_ref.shape[2]
    for peer in range(peers):

        @pl.when(step == peer)
        def _(peer=peer):
            product = lax.dot_general(
                dense_ref[...], backs[peer][...], (((0,), (0,)), ((), ())), preferred_element_type=F32
            )
            if peer == 0:
                total[...] = product
            else:
                total[...] += product

    @pl.when(step == peers - 1)
    def _():
        for slot in range(slots):
            rows = total[slot * capacity : (slot + 1) * capacity, :].astype(BF16)
            outs[slot][...] = jnp.dot(put_ref[slot], rows, preferred_element_type=F32).astype(
                outs[slot].dtype
            )


def backward_blocks(dense, put, backs, pos, kept):
    peers = len(backs)
    rows, width = dense.shape
    slots, nodes, _ = put.shape
    chunk = backs[0].shape[1]
    block = rows // peers
    return pl.pallas_call(
        functools.partial(backward_blocks_kernel, peers, slots),
        out_shape=tuple(
            jax.ShapeDtypeStruct((nodes, chunk), F32 if slot in kept else BF16)
            for slot in range(slots)
        ),
        grid_spec=pltpu.PrefetchScalarGridSpec(
            num_scalar_prefetch=1,
            grid=(peers,),
            in_specs=[
                full_spec(put.shape),
                pl.BlockSpec((block, width), lambda i, pos_ref: (i ^ pos_ref[0], 0)),
            ]
            + [full_spec((block, chunk))] * peers,
            out_specs=tuple(full_spec((nodes, chunk)) for _ in range(slots)),
            scratch_shapes=[pltpu.VMEM((width, chunk), F32)],
        ),
        compiler_params=params(BIG_LIMIT),
        cost_estimate=pl.CostEstimate(
            flops=2 * rows * width * chunk, bytes_accessed=2 * rows * width, transcendentals=0
        ),
        name="backward_rows",
    )(pos, put, dense, *backs)


def pair_sum_kernel(count, *refs):
    for i in range(count):
        total = refs[i][...].astype(F32) + refs[count + i][...].astype(F32)
        refs[2 * count + i][...] = total.astype(refs[2 * count + i].dtype)


def pair_sums(kept, received, wide=-1):
    count = len(kept)
    return pl.pallas_call(
        functools.partial(pair_sum_kernel, count),
        out_shape=tuple(
            jax.ShapeDtypeStruct(kept[i].shape, F32 if i == wide else BF16) for i in range(count)
        ),
        compiler_params=params(),
        cost_estimate=pl.CostEstimate(
            flops=0, bytes_accessed=count * kept[0].size * 8, transcendentals=0
        ),
        name="pair_sums",
    )(*kept, *received)


def finish_kernel(chunks, each, *refs):
    out_ref = refs[-1]
    size = out_ref.shape[1] // chunks
    for chunk in range(chunks):
        total = refs[chunk * each][...].astype(F32)
        for term in range(1, each):
            total = total + refs[chunk * each + term][...].astype(F32)
        out_ref[:, chunk * size : (chunk + 1) * size] = total.astype(BF16)


def finish(terms):
    chunks, each = len(terms), len(terms[0])
    nodes, size = terms[0][0].shape
    return pl.pallas_call(
        functools.partial(finish_kernel, chunks, each),
        out_shape=jax.ShapeDtypeStruct((nodes, size * chunks), BF16),
        compiler_params=params(),
        cost_estimate=pl.CostEstimate(
            flops=0, bytes_accessed=chunks * nodes * size * 2 * each, transcendentals=0
        ),
        name="finish",
    )(*[array for group in terms for array in group])


LINE_SWAP1 = z_pairs([(0, 1), (1, 0), (2, 3), (3, 2)])
LINE_SWAP2 = z_pairs([(0, 2), (2, 0), (1, 3), (3, 1)])
LINE_MIDDLE = z_pairs([(1, 2), (2, 1)])
LINE_OUT = z_pairs([(2, 3), (1, 0)])
LINE_IN = z_pairs([(3, 2), (0, 1)])
CORE = xor_pairs(8, 1)


def after(value, *others):
    return lax.optimization_barrier((value,) + others)[0]


def exchange_add(value, axis, size, step):
    return value + lax.ppermute(value, axis, xor_pairs(size, step))


def with_lists(features, list_rows, list_counts):
    live = jnp.arange(list_rows.shape[1])[None, :] < list_counts[:, None]
    high = jnp.where(live, list_rows // 256, -1)
    low = jnp.where(live, list_rows % 256, 0)
    return jnp.concatenate([features, high.astype(BF16), low.astype(BF16)], axis=0)


def line_exchange(piece, dense_of, pos, nodes, capacity, rows):
    far = lax.ppermute(piece, "col", LINE_SWAP2)
    near = lax.ppermute(piece, "col", LINE_SWAP1)
    other = lax.ppermute(piece, "col", CORE)
    dense = dense_of()
    far, dense = lax.optimization_barrier((far, dense))
    ends = lax.ppermute(far, "col", LINE_OUT)
    middle = lax.ppermute(after(piece, far), "col", LINE_MIDDLE)
    early = [[piece], [other], [near], [lax.ppermute(far, "col", CORE)], [far]]
    partial, put_early = forward_part(dense, early, 0, pos, rows, nodes, capacity)
    partial, middle, ends = lax.optimization_barrier((partial, middle, ends))
    other = [lax.ppermute(middle, "col", CORE), lax.ppermute(ends, "col", CORE)]
    late = [[lax.ppermute(near, "col", CORE)], [middle, ends]]
    partial, put_late = forward_part(dense, late, 5, pos, rows, nodes, capacity, partial)
    *blocks, put_last = forward_part(
        dense, [other], 7, pos, rows, nodes, capacity, partial, True
    )
    return dense, (put_early, put_late, put_last), blocks


def row_exchange(own, arrays, rows):
    received = [
        lax.ppermute(arrays[step - 1], "row", xor_pairs(rows, step))
        for step in reversed(range(1, rows))
    ]
    return [own] + received[::-1]


def line_reduce(dense, puts, back, backs, sums, rows, columns):
    put_early, put_late, put_last = puts
    first = backward_early(dense, back)
    sums = sums + after(lax.ppermute(sums, "col", xor_pairs(columns, 4)), backs[2])
    sums = exchange_add(sums, "col", columns, 2)
    *backs, first, sums = lax.optimization_barrier((*backs, first, sums))
    keep3, give3 = backward_late(
        dense, (put_late, put_last), ((1,), (0,)), first, backs, 6
    )
    got3 = lax.ppermute(give3, "col", CORE)
    received = lax.ppermute(sums, "row", xor_pairs(rows, 1))
    keep0, give0, keep1, give2, keep2, give1 = backward_late(
        dense, (put_early, put_late), (tuple(range(5)), (0,)), first, backs, 0
    )
    got3, give2, give1, give0, keep0 = lax.optimization_barrier((got3, give2, give1, give0, keep0))
    (last,) = pair_sums([keep3], [got3])
    passed = lax.ppermute(last, "col", LINE_IN)
    middle = lax.ppermute(last, "col", LINE_MIDDLE)
    got = [lax.ppermute(give, "col", CORE) for give in (give0, give1, give2)]
    own, near, far = pair_sums([keep0, keep1, keep2], got, 0)
    sums = sums + after(received, own)
    step = 2
    while step < rows:
        sums = exchange_add(sums, "row", rows, step)
        step *= 2
    passed, middle = lax.optimization_barrier((passed, middle))
    far = (far.astype(F32) + passed.astype(F32)).astype(BF16)
    from_far = lax.ppermute(far, "col", LINE_SWAP2)
    near, sums = lax.optimization_barrier((near, sums))
    from_near = lax.ppermute(after(near, far), "col", LINE_SWAP1)
    return [own, middle, from_near, from_far], sums


def per_device(
    features,
    weight,
    bias_vector,
    send_rows,
    send_count,
    adjacency,
    source_tile,
    tile_count,
    cotangent,
):
    rows, columns = lax.axis_size("row"), lax.axis_size("col")
    nodes, width = features.shape
    capacity = send_rows.shape[3]
    tiles, source, count = adjacency[0, 0], source_tile[0, 0], tile_count[0, 0]
    pos = jnp.stack([lax.axis_index("row"), lax.axis_index("col")]).astype(jnp.int32)
    piece = with_lists(features, send_rows[0, 0], send_count[0, 0])
    line = columns == 8 and 2 * tiles.shape[0] * TILE * columns * capacity <= RESIDENT

    if line:
        dense, puts, blocks = line_exchange(
            piece,
            lambda: densify(tiles, source, count, pos, rows, columns, capacity),
            pos,
            nodes,
            capacity,
            rows,
        )
    else:
        dense = densify_blocks(tiles, source, count, pos, columns, capacity)
        pieces = [piece] + [
            lax.ppermute(piece, "col", xor_pairs(columns, step)) for step in range(1, columns)
        ]
        here = lax.axis_index("col")
        lists = jnp.stack(
            [
                list_row(
                    lax.dynamic_index_in_dim(a, nodes + here, 0, keepdims=False),
                    lax.dynamic_index_in_dim(a, nodes + columns + here, 0, keepdims=False),
                )
                for a in pieces
            ]
        )
        pick, put = selectors(lists, nodes)
        blocks = forward_blocks(dense, pick, [[a[:nodes]] for a in pieces], pos, rows)

    parts = row_exchange(blocks[0], blocks[1:], rows)
    scale = 1.0 / math.sqrt(nodes * rows * columns)
    output, back, mine, theirs = layer(weight, bias_vector, cotangent, parts, pos, scale)
    backs = row_exchange(back, [back] * (rows - 1), rows)
    sums = mine + lax.ppermute(theirs, "col", CORE if line else xor_pairs(columns, 1))

    if line:
        terms, sums = line_reduce(
            dense, puts, back, backs[1:], sums, rows, columns
        )
    else:
        scattered = backward_blocks(dense, put, backs, pos, (0,))
        terms = [scattered[0]] + [
            lax.ppermute(scattered[step], "col", xor_pairs(columns, step))
            for step in range(1, columns)
        ]
        step = 2
        while step < columns:
            sums = exchange_add(sums, "col", columns, step)
            step *= 2
        step = 1
        while step < rows:
            sums = exchange_add(sums, "row", rows, step)
            step *= 2
    weight_grad, bias_grad = assemble(
        sums, lax.ppermute(sums, "col", xor_pairs(columns, 1)), pos
    )
    terms[-1], weight_grad, bias_grad = lax.optimization_barrier(
        (terms[-1], weight_grad, bias_grad)
    )
    return output, finish([terms]), weight_grad, bias_grad


def solution(mesh):
    in_specs = (
        P(("row", "col"), None),
        P(),
        P(),
        P("row", "col", None, None),
        P("row", "col", None),
        P("row", "col", None, None, None, None),
        P("row", "col", None, None),
        P("row", "col", None),
        P(("row", "col"), None),
    )
    out_specs = (P(("row", "col"), None), P(("row", "col"), None), P(), P())
    return jax.shard_map(
        per_device, mesh=mesh, in_specs=in_specs, out_specs=out_specs, check_vma=False
    )
```

```python
import functools
import math

import jax
import jax.numpy as jnp
from jax import lax
from jax.experimental import pallas as pl
from jax.experimental.pallas import tpu as pltpu
from jax.sharding import PartitionSpec as P

TILE = 128
VMEM_LIMIT = 16 * 1024 * 1024
BIG_LIMIT = 40 * 1024 * 1024
RESIDENT = 16 * 1024 * 1024
BF16 = jnp.bfloat16
F32 = jnp.float32


def full_spec(shape):
    return pl.BlockSpec(shape, lambda *_: (0,) * len(shape))


def params(limit=VMEM_LIMIT):
    return pltpu.CompilerParams(vmem_limit_bytes=limit)


def xor_pairs(size, step):
    return [(i, i ^ step) for i in range(size)]


def z_pairs(pairs):
    return [(2 * a + core, 2 * b + core) for a, b in pairs for core in range(2)]


def densify_kernel(per_piece, per_peer, src_ref, cnt_ref, pos_ref, adj_ref, out_ref, held, sems):
    targets, slots = adj_ref.shape[0], adj_ref.shape[1]
    here = pos_ref[1]
    whole = slots * TILE == out_ref.shape[1]
    copies = [
        pltpu.make_async_copy(adj_ref.at[t], held.at[t], sems.at[t]) for t in range(targets)
    ]
    for copy in copies:
        copy.start()
    for t, copy in enumerate(copies):
        block = ((t // per_peer) ^ pos_ref[0]) * per_peer + t % per_peer
        rows = pl.ds(pl.multiple_of(block * TILE, TILE), TILE)
        if not whole:
            out_ref[rows, :] = jnp.zeros((TILE, out_ref.shape[1]), out_ref.dtype)
        count = cnt_ref[t]
        copy.wait()
        for s in range(slots):
            source = src_ref[t, s]
            slot = (source // per_piece) ^ here
            place = jnp.where((slot == 3) | (slot == 5), slot ^ 6, slot)
            column = pl.multiple_of((place * per_piece + source % per_piece) * TILE, TILE)
            tile = held[t, s]
            out_ref[rows, pl.ds(column, TILE)] = jnp.where(s < count, tile, jnp.zeros_like(tile))


def densify(adjacency, source_tile, tile_count, pos, peers, pieces, capacity):
    targets = adjacency.shape[0]
    width = pieces * capacity
    smem = pl.BlockSpec(memory_space=pltpu.SMEM)
    return pl.pallas_call(
        functools.partial(densify_kernel, capacity // TILE, targets // peers),
        out_shape=jax.ShapeDtypeStruct((targets * TILE, width), BF16),
        in_specs=[smem, smem, smem, pl.BlockSpec(memory_space=pl.ANY)],
        out_specs=pl.BlockSpec(memory_space=pltpu.VMEM),
        scratch_shapes=[
            pltpu.VMEM(adjacency.shape, BF16),
            pltpu.SemaphoreType.DMA((targets,)),
        ],
        compiler_params=params(40 * 1024 * 1024),
        cost_estimate=pl.CostEstimate(
            flops=0, bytes_accessed=4 * targets * TILE * width, transcendentals=0
        ),
        name="densify",
    )(source_tile, tile_count, pos, adjacency)


def densify_blocks_kernel(per_piece, src_ref, cnt_ref, pos_ref, adj_ref, out_ref):
    step = pl.program_id(0)
    tiles, slots = adj_ref.shape[0], adj_ref.shape[1]
    out_ref[...] = jnp.zeros_like(out_ref)
    here = pos_ref[1]
    for t in range(tiles):
        count = cnt_ref[step * tiles + t]
        for s in range(slots):

            @pl.when(s < count)
            def _(t=t, s=s):
                source = src_ref[step * tiles + t, s]
                slot = (source // per_piece) ^ here
                column = pl.multiple_of((slot * per_piece + source % per_piece) * TILE, TILE)
                out_ref[t * TILE : (t + 1) * TILE, pl.ds(column, TILE)] = adj_ref[t, s]


def densify_blocks(adjacency, source_tile, tile_count, pos, pieces, capacity):
    targets, slots = adjacency.shape[0], adjacency.shape[1]
    tiles = 4
    width = pieces * capacity
    return pl.pallas_call(
        functools.partial(densify_blocks_kernel, capacity // TILE),
        out_shape=jax.ShapeDtypeStruct((targets * TILE, width), BF16),
        grid_spec=pltpu.PrefetchScalarGridSpec(
            num_scalar_prefetch=3,
            grid=(targets // tiles,),
            in_specs=[pl.BlockSpec((tiles, slots, TILE, TILE), lambda i, *_: (i, 0, 0, 0))],
            out_specs=pl.BlockSpec((tiles * TILE, width), lambda i, *_: (i, 0)),
        ),
        compiler_params=params(BIG_LIMIT),
        cost_estimate=pl.CostEstimate(
            flops=0, bytes_accessed=2 * targets * TILE * (width + slots * TILE), transcendentals=0
        ),
        name="densify",
    )(source_tile, tile_count, pos, adjacency)


def hits(row, nodes):
    node = lax.broadcasted_iota(jnp.int32, (nodes, row.shape[1]), 0).astype(F32)
    return jnp.where(node == row, 1.0, 0.0).astype(BF16)


def list_row(high, low):
    return high.astype(F32) * 256.0 + low.astype(F32)


def select_kernel(list_ref, pick_ref, put_ref):
    slots, nodes, _ = put_ref.shape
    for slot in range(slots):
        put = hits(list_ref[slot : slot + 1, :], nodes)
        put_ref[slot] = put
        pick_ref[slot] = put.T


def selectors(lists, nodes):
    pieces, capacity = lists.shape
    return pl.pallas_call(
        select_kernel,
        out_shape=(
            jax.ShapeDtypeStruct((pieces, capacity, nodes), BF16),
            jax.ShapeDtypeStruct((pieces, nodes, capacity), BF16),
        ),
        compiler_params=params(BIG_LIMIT),
        cost_estimate=pl.CostEstimate(
            flops=0, bytes_accessed=4 * pieces * capacity * nodes, transcendentals=0
        ),
        name="selectors",
    )(lists)


def gather_rows(sources, here, put_ref, at):
    nodes, capacity = put_ref.shape[1:]
    columns = (sources[0].shape[0] - nodes) // 2
    piece = sources[0][:nodes, :]
    tail = sources[0][nodes:, :].astype(F32)
    for extra in sources[1:]:
        piece = piece + extra[:nodes, :]
        tail = tail + extra[nodes:, :].astype(F32)
    table = list_row(tail[:columns], tail[columns:])
    mine = lax.broadcasted_iota(jnp.int32, table.shape, 0) == here
    put = hits(jnp.sum(jnp.where(mine, table, 0.0), axis=0, keepdims=True), nodes)
    put_ref[at] = put
    rows = lax.dot_general(put, piece, (((0,), (0,)), ((), ())), preferred_element_type=F32)
    return rows.astype(BF16)


def forward_part_kernel(groups, base, peers, added, last, pos_ref, dense_ref, *rest):
    total = sum(groups)
    sources, rest = rest[:total], list(rest[total:])
    before_ref = rest.pop(0) if added else None
    *outs, put_ref, gathered = rest
    here = pos_ref[1]
    capacity = put_ref.shape[2]
    at = 0
    for slot, count in enumerate(groups):
        rows = gather_rows(sources[at : at + count], here, put_ref, slot)
        gathered[slot * capacity : (slot + 1) * capacity, :] = rows
        at += count
    columns = slice(base * capacity, (base + len(groups)) * capacity)
    block = dense_ref.shape[0] // peers
    for peer in range(peers):
        here_rows = slice(peer * block, (peer + 1) * block)
        result = jnp.dot(
            dense_ref[here_rows, columns], gathered[...], preferred_element_type=F32
        )
        if added:
            result = before_ref[here_rows, :] + result
        if last:
            outs[peer][...] = result.astype(outs[peer].dtype)
        else:
            outs[0][here_rows, :] = result


def forward_part(dense, groups, base, pos, peers, nodes, capacity, before=None, last=False):
    rows = dense.shape[0]
    flat = [array for group in groups for array in group]
    width = flat[0].shape[1]
    added = before is not None
    if last:
        outs = tuple(
            jax.ShapeDtypeStruct((rows // peers, width), F32 if peer == 0 else BF16)
            for peer in range(peers)
        )
    else:
        outs = (jax.ShapeDtypeStruct((rows, width), F32),)
    depth = len(groups) * capacity
    if added:
        flat = flat + [before]
    return pl.pallas_call(
        functools.partial(
            forward_part_kernel, tuple(len(group) for group in groups), base, peers, added, last
        ),
        out_shape=outs + (jax.ShapeDtypeStruct((len(groups), nodes, capacity), BF16),),
        in_specs=[pl.BlockSpec(memory_space=pltpu.SMEM)]
        + [pl.BlockSpec(memory_space=pltpu.VMEM)] * (1 + len(flat)),
        scratch_shapes=[pltpu.VMEM((depth, width), BF16)],
        compiler_params=params(),
        cost_estimate=pl.CostEstimate(
            flops=2 * rows * depth * width, bytes_accessed=2 * rows * depth, transcendentals=0
        ),
        name="forward_last" if last else "forward_part",
    )(pos, dense, *flat)


def forward_blocks_kernel(groups, peers, pos_ref, pick_ref, dense_ref, *rest):
    total = sum(groups)
    sources, outs, gathered = rest[:total], rest[total : total + peers], rest[total + peers]
    step = pl.program_id(0)
    capacity = pick_ref.shape[1]

    @pl.when(step == 0)
    def _():
        at = 0
        for slot, count in enumerate(groups):
            piece = sources[at][...]
            for extra in range(1, count):
                piece = piece + sources[at + extra][...]
            at += count
            rows = jnp.dot(pick_ref[slot], piece, preferred_element_type=F32)
            gathered[slot * capacity : (slot + 1) * capacity, :] = rows.astype(BF16)

    result = jnp.dot(dense_ref[...], gathered[...], preferred_element_type=F32)
    for peer in range(peers):

        @pl.when(step == peer)
        def _(peer=peer):
            outs[peer][...] = result.astype(outs[peer].dtype)


def forward_blocks(dense, pick, groups, pos, peers):
    rows, width = dense.shape
    flat = [array for group in groups for array in group]
    nodes, chunk = flat[0].shape
    block = rows // peers
    return pl.pallas_call(
        functools.partial(forward_blocks_kernel, tuple(len(group) for group in groups), peers),
        out_shape=tuple(
            jax.ShapeDtypeStruct((block, chunk), F32 if peer == 0 else BF16)
            for peer in range(peers)
        ),
        grid_spec=pltpu.PrefetchScalarGridSpec(
            num_scalar_prefetch=1,
            grid=(peers,),
            in_specs=[
                full_spec(pick.shape),
                pl.BlockSpec((block, width), lambda i, pos_ref: (i ^ pos_ref[0], 0)),
            ]
            + [full_spec((nodes, chunk))] * len(flat),
            out_specs=tuple(full_spec((block, chunk)) for _ in range(peers)),
            scratch_shapes=[pltpu.VMEM((width, chunk), BF16)],
        ),
        compiler_params=params(BIG_LIMIT),
        cost_estimate=pl.CostEstimate(
            flops=2 * rows * width * chunk, bytes_accessed=2 * rows * width, transcendentals=0
        ),
        name="forward_rows",
    )(pos, pick, dense, *flat)


def layer_kernel(peers, scale, pos_ref, weight_ref, bias_ref, cot_ref, *rest):
    parts, (out_ref, back_ref, mine_ref, theirs_ref) = rest[:peers], rest[peers:]
    total = parts[0][...].astype(F32)
    for peer in range(1, peers):
        total = total + parts[peer][...].astype(F32)
    agg = total.astype(BF16)
    weight = weight_ref[...]
    preact = jnp.dot(agg, weight, preferred_element_type=F32) + bias_ref[...]
    sigma = 1.0 / (1.0 + jnp.exp(-preact))
    out_ref[...] = (preact * sigma).astype(BF16)
    grad = (cot_ref[...].astype(F32) * sigma * (1.0 + preact * (1.0 - sigma))).astype(BF16)
    back_ref[...] = lax.dot_general(
        grad, weight, (((1,), (1,)), ((), ())), preferred_element_type=F32
    ).astype(BF16)
    product = scale * lax.dot_general(
        agg, grad, (((0,), (0,)), ((), ())), preferred_element_type=F32
    )
    bias = scale * jnp.sum(grad.astype(F32).reshape(-1, 8, grad.shape[1]), axis=0)
    half = product.shape[0] // 2
    core = pos_ref[1] % 2
    for keep, give, parity in ((mine_ref, theirs_ref, 0), (theirs_ref, mine_ref, 1)):

        @pl.when(core == parity)
        def _(keep=keep, give=give):
            keep[:half] = product[:half]
            give[:half] = product[half:]

    mine_ref[half:] = bias
    theirs_ref[half:] = bias


def layer(weight, bias_vector, cotangent, parts, pos, scale):
    nodes, width = cotangent.shape
    return pl.pallas_call(
        functools.partial(layer_kernel, len(parts), scale),
        out_shape=(jax.ShapeDtypeStruct((nodes, width), BF16),) * 2
        + (jax.ShapeDtypeStruct((width // 2 + 8, width), F32),) * 2,
        in_specs=[pl.BlockSpec(memory_space=pltpu.SMEM)]
        + [pl.BlockSpec(memory_space=pltpu.VMEM)] * (3 + len(parts)),
        compiler_params=params(),
        cost_estimate=pl.CostEstimate(
            flops=6 * nodes * width * width,
            bytes_accessed=2 * nodes * width * 10,
            transcendentals=nodes * width,
        ),
        name="layer",
    )(pos, weight, bias_vector.reshape(1, -1), cotangent, *parts)


def assemble_kernel(pos_ref, mine_ref, theirs_ref, weight_ref, bias_ref):
    half = weight_ref.shape[0] // 2
    core = pos_ref[1] % 2
    mine = pl.multiple_of(core * half, half)
    theirs = pl.multiple_of((1 - core) * half, half)
    weight_ref[pl.ds(mine, half), :] = mine_ref[:half]
    weight_ref[pl.ds(theirs, half), :] = theirs_ref[:half]
    bias_ref[...] = jnp.sum(mine_ref[half:], axis=0, keepdims=True)


def assemble(mine, theirs, pos):
    width = mine.shape[1]
    weight, bias = pl.pallas_call(
        assemble_kernel,
        out_shape=(
            jax.ShapeDtypeStruct((width, width), F32),
            jax.ShapeDtypeStruct((1, width), F32),
        ),
        in_specs=[pl.BlockSpec(memory_space=pltpu.SMEM)]
        + [pl.BlockSpec(memory_space=pltpu.VMEM)] * 2,
        compiler_params=params(),
        cost_estimate=pl.CostEstimate(
            flops=0, bytes_accessed=16 * width * width, transcendentals=0
        ),
        name="assemble",
    )(pos, mine, theirs)
    return weight, bias.reshape(width)


def back_product(dense, back):
    return lax.dot_general(
        dense, back, (((0,), (0,)), ((), ())), preferred_element_type=F32
    )


def backward_early_kernel(dense_ref, back_ref, out_ref):
    out_ref[...] = back_product(dense_ref[: back_ref.shape[0], :], back_ref[...])


def backward_early(dense, back):
    width, size = dense.shape[1], back.shape[1]
    return pl.pallas_call(
        backward_early_kernel,
        out_shape=jax.ShapeDtypeStruct((width, size), F32),
        compiler_params=params(),
        cost_estimate=pl.CostEstimate(
            flops=2 * width * back.size, bytes_accessed=6 * width * size, transcendentals=0
        ),
        name="backward_early",
    )(dense, back)


def backward_late_kernel(base, slots, peers, dense_ref, *rest):
    puts, rest = rest[: len(slots)], rest[len(slots) :]
    first_ref, rest = rest[0], rest[1:]
    backs, outs, (joined, rows) = rest[: peers - 1], rest[peers - 1 : -2], rest[-2:]
    capacity = puts[0].shape[2]
    block = backs[0].shape[0]
    for peer in range(1, peers):
        joined[(peer - 1) * block : peer * block, :] = backs[peer - 1][...]
    columns = slice(base * capacity, (base + len(outs)) * capacity)
    rows[...] = (
        first_ref[columns, :] + back_product(dense_ref[block:, columns], joined[...])
    ).astype(BF16)
    at = 0
    for put_ref, picked in zip(puts, slots):
        for slot in picked:
            outs[at][...] = jnp.dot(
                put_ref[slot],
                rows[at * capacity : (at + 1) * capacity, :],
                preferred_element_type=F32,
            ).astype(outs[at].dtype)
            at += 1


def backward_late(dense, puts, slots, first, backs, base):
    _, nodes, capacity = puts[0].shape
    count = sum(len(picked) for picked in slots)
    size = first.shape[1]
    return pl.pallas_call(
        functools.partial(backward_late_kernel, base, slots, len(backs) + 1),
        out_shape=tuple(
            jax.ShapeDtypeStruct((nodes, size), BF16 if (base + at) % 2 else F32)
            for at in range(count)
        ),
        scratch_shapes=[
            pltpu.VMEM((len(backs) * backs[0].shape[0], size), BF16),
            pltpu.VMEM((count * capacity, size), BF16),
        ],
        compiler_params=params(),
        cost_estimate=pl.CostEstimate(
            flops=2 * count * capacity * size * dense.shape[0],
            bytes_accessed=2 * dense.shape[0] * count * capacity,
            transcendentals=0,
        ),
        name="backward_late",
    )(dense, *puts, first, *backs)


def backward_blocks_kernel(peers, slots, pos_ref, put_ref, dense_ref, *rest):
    backs, outs, total = rest[:peers], rest[peers : peers + slots], rest[peers + slots]
    step = pl.program_id(0)
    capacity = put_ref.shape[2]
    for peer in range(peers):

        @pl.when(step == peer)
        def _(peer=peer):
            product = lax.dot_general(
                dense_ref[...], backs[peer][...], (((0,), (0,)), ((), ())), preferred_element_type=F32
            )
            if peer == 0:
                total[...] = product
            else:
                total[...] += product

    @pl.when(step == peers - 1)
    def _():
        for slot in range(slots):
            rows = total[slot * capacity : (slot + 1) * capacity, :].astype(BF16)
            outs[slot][...] = jnp.dot(put_ref[slot], rows, preferred_element_type=F32).astype(
                outs[slot].dtype
            )


def backward_blocks(dense, put, backs, pos, kept):
    peers = len(backs)
    rows, width = dense.shape
    slots, nodes, _ = put.shape
    chunk = backs[0].shape[1]
    block = rows // peers
    return pl.pallas_call(
        functools.partial(backward_blocks_kernel, peers, slots),
        out_shape=tuple(
            jax.ShapeDtypeStruct((nodes, chunk), F32 if slot in kept else BF16)
            for slot in range(slots)
        ),
        grid_spec=pltpu.PrefetchScalarGridSpec(
            num_scalar_prefetch=1,
            grid=(peers,),
            in_specs=[
                full_spec(put.shape),
                pl.BlockSpec((block, width), lambda i, pos_ref: (i ^ pos_ref[0], 0)),
            ]
            + [full_spec((block, chunk))] * peers,
            out_specs=tuple(full_spec((nodes, chunk)) for _ in range(slots)),
            scratch_shapes=[pltpu.VMEM((width, chunk), F32)],
        ),
        compiler_params=params(BIG_LIMIT),
        cost_estimate=pl.CostEstimate(
            flops=2 * rows * width * chunk, bytes_accessed=2 * rows * width, transcendentals=0
        ),
        name="backward_rows",
    )(pos, put, dense, *backs)


def pair_sum_kernel(count, *refs):
    for i in range(count):
        total = refs[i][...].astype(F32) + refs[count + i][...].astype(F32)
        refs[2 * count + i][...] = total.astype(refs[2 * count + i].dtype)


def pair_sums(kept, received, wide=-1):
    count = len(kept)
    return pl.pallas_call(
        functools.partial(pair_sum_kernel, count),
        out_shape=tuple(
            jax.ShapeDtypeStruct(kept[i].shape, F32 if i == wide else BF16) for i in range(count)
        ),
        compiler_params=params(),
        cost_estimate=pl.CostEstimate(
            flops=0, bytes_accessed=count * kept[0].size * 8, transcendentals=0
        ),
        name="pair_sums",
    )(*kept, *received)


def finish_kernel(chunks, each, *refs):
    out_ref = refs[-1]
    size = out_ref.shape[1] // chunks
    for chunk in range(chunks):
        total = refs[chunk * each][...].astype(F32)
        for term in range(1, each):
            total = total + refs[chunk * each + term][...].astype(F32)
        out_ref[:, chunk * size : (chunk + 1) * size] = total.astype(BF16)


def finish(terms):
    chunks, each = len(terms), len(terms[0])
    nodes, size = terms[0][0].shape
    return pl.pallas_call(
        functools.partial(finish_kernel, chunks, each),
        out_shape=jax.ShapeDtypeStruct((nodes, size * chunks), BF16),
        compiler_params=params(),
        cost_estimate=pl.CostEstimate(
            flops=0, bytes_accessed=chunks * nodes * size * 2 * each, transcendentals=0
        ),
        name="finish",
    )(*[array for group in terms for array in group])


LINE_SWAP1 = z_pairs([(0, 1), (1, 0), (2, 3), (3, 2)])
LINE_SWAP2 = z_pairs([(0, 2), (2, 0), (1, 3), (3, 1)])
LINE_MIDDLE = z_pairs([(1, 2), (2, 1)])
LINE_OUT = z_pairs([(2, 3), (1, 0)])
LINE_IN = z_pairs([(3, 2), (0, 1)])
CORE = xor_pairs(8, 1)


def after(value, *others):
    return lax.optimization_barrier((value,) + others)[0]


def exchange_add(value, axis, size, step):
    return value + lax.ppermute(value, axis, xor_pairs(size, step))


def with_lists(features, list_rows, list_counts):
    live = jnp.arange(list_rows.shape[1])[None, :] < list_counts[:, None]
    high = jnp.where(live, list_rows // 256, -1)
    low = jnp.where(live, list_rows % 256, 0)
    return jnp.concatenate([features, high.astype(BF16), low.astype(BF16)], axis=0)


def line_exchange(piece, dense_of, pos, nodes, capacity, rows):
    far = lax.ppermute(piece, "col", LINE_SWAP2)
    near = lax.ppermute(piece, "col", LINE_SWAP1)
    other = lax.ppermute(piece, "col", CORE)
    dense = dense_of()
    far, dense = lax.optimization_barrier((far, dense))
    ends = lax.ppermute(far, "col", LINE_OUT)
    middle = lax.ppermute(after(piece, far), "col", LINE_MIDDLE)
    early = [[piece], [other], [near], [lax.ppermute(far, "col", CORE)], [far]]
    partial, put_early = forward_part(dense, early, 0, pos, rows, nodes, capacity)
    partial, middle, ends = lax.optimization_barrier((partial, middle, ends))
    other = [lax.ppermute(middle, "col", CORE), lax.ppermute(ends, "col", CORE)]
    late = [[lax.ppermute(near, "col", CORE)], [middle, ends]]
    partial, put_late = forward_part(dense, late, 5, pos, rows, nodes, capacity, partial)
    *blocks, put_last = forward_part(
        dense, [other], 7, pos, rows, nodes, capacity, partial, True
    )
    return dense, (put_early, put_late, put_last), blocks


def row_exchange(own, arrays, rows):
    received = [
        lax.ppermute(arrays[step - 1], "row", xor_pairs(rows, step))
        for step in reversed(range(1, rows))
    ]
    return [own] + received[::-1]


def line_reduce(dense, puts, back, backs, sums, rows, columns):
    put_early, put_late, put_last = puts
    first = backward_early(dense, back)
    sums = sums + after(lax.ppermute(sums, "col", xor_pairs(columns, 4)), backs[2])
    sums = exchange_add(sums, "col", columns, 2)
    *backs, first, sums = lax.optimization_barrier((*backs, first, sums))
    keep3, give3 = backward_late(
        dense, (put_late, put_last), ((1,), (0,)), first, backs, 6
    )
    got3 = lax.ppermute(give3, "col", CORE)
    received = lax.ppermute(sums, "row", xor_pairs(rows, 1))
    keep0, give0, keep1, give2, keep2, give1 = backward_late(
        dense, (put_early, put_late), (tuple(range(5)), (0,)), first, backs, 0
    )
    got3, give2, give1, give0, keep0 = lax.optimization_barrier((got3, give2, give1, give0, keep0))
    (last,) = pair_sums([keep3], [got3])
    passed = lax.ppermute(last, "col", LINE_IN)
    middle = lax.ppermute(last, "col", LINE_MIDDLE)
    got = [lax.ppermute(give, "col", CORE) for give in (give0, give1, give2)]
    own, near, far = pair_sums([keep0, keep1, keep2], got, 0)
    from_near = lax.ppermute(near, "col", LINE_SWAP1)
    sums = sums + after(received, own)
    step = 2
    while step < rows:
        sums = exchange_add(sums, "row", rows, step)
        step *= 2
    far = (far.astype(F32) + passed.astype(F32)).astype(BF16)
    from_far = lax.ppermute(far, "col", LINE_SWAP2)
    middle, sums = lax.optimization_barrier((middle, sums))
    sums = after(sums, from_near)
    return [own, middle, from_near, from_far], sums


def per_device(
    features,
    weight,
    bias_vector,
    send_rows,
    send_count,
    adjacency,
    source_tile,
    tile_count,
    cotangent,
):
    rows, columns = lax.axis_size("row"), lax.axis_size("col")
    nodes, width = features.shape
    capacity = send_rows.shape[3]
    tiles, source, count = adjacency[0, 0], source_tile[0, 0], tile_count[0, 0]
    pos = jnp.stack([lax.axis_index("row"), lax.axis_index("col")]).astype(jnp.int32)
    piece = with_lists(features, send_rows[0, 0], send_count[0, 0])
    line = columns == 8 and 2 * tiles.shape[0] * TILE * columns * capacity <= RESIDENT

    if line:
        dense, puts, blocks = line_exchange(
            piece,
            lambda: densify(tiles, source, count, pos, rows, columns, capacity),
            pos,
            nodes,
            capacity,
            rows,
        )
    else:
        dense = densify_blocks(tiles, source, count, pos, columns, capacity)
        pieces = [piece] + [
            lax.ppermute(piece, "col", xor_pairs(columns, step)) for step in range(1, columns)
        ]
        here = lax.axis_index("col")
        lists = jnp.stack(
            [
                list_row(
                    lax.dynamic_index_in_dim(a, nodes + here, 0, keepdims=False),
                    lax.dynamic_index_in_dim(a, nodes + columns + here, 0, keepdims=False),
                )
                for a in pieces
            ]
        )
        pick, put = selectors(lists, nodes)
        blocks = forward_blocks(dense, pick, [[a[:nodes]] for a in pieces], pos, rows)

    parts = row_exchange(blocks[0], blocks[1:], rows)
    scale = 1.0 / math.sqrt(nodes * rows * columns)
    output, back, mine, theirs = layer(weight, bias_vector, cotangent, parts, pos, scale)
    backs = row_exchange(back, [back] * (rows - 1), rows)
    sums = mine + lax.ppermute(theirs, "col", CORE if line else xor_pairs(columns, 1))

    if line:
        terms, sums = line_reduce(
            dense, puts, back, backs[1:], sums, rows, columns
        )
    else:
        scattered = backward_blocks(dense, put, backs, pos, (0,))
        terms = [scattered[0]] + [
            lax.ppermute(scattered[step], "col", xor_pairs(columns, step))
            for step in range(1, columns)
        ]
        step = 2
        while step < columns:
            sums = exchange_add(sums, "col", columns, step)
            step *= 2
        step = 1
        while step < rows:
            sums = exchange_add(sums, "row", rows, step)
            step *= 2
    weight_grad, bias_grad = assemble(
        sums, lax.ppermute(sums, "col", xor_pairs(columns, 1)), pos
    )
    terms[-1], weight_grad, bias_grad = lax.optimization_barrier(
        (terms[-1], weight_grad, bias_grad)
    )
    return output, finish([terms]), weight_grad, bias_grad


def solution(mesh):
    in_specs = (
        P(("row", "col"), None),
        P(),
        P(),
        P("row", "col", None, None),
        P("row", "col", None),
        P("row", "col", None, None, None, None),
        P("row", "col", None, None),
        P("row", "col", None),
        P(("row", "col"), None),
    )
    out_specs = (P(("row", "col"), None), P(("row", "col"), None), P(), P())
    return jax.shard_map(
        per_device, mesh=mesh, in_specs=in_specs, out_specs=out_specs, check_vma=False
    )
```

```python
import functools
import math

import jax
import jax.numpy as jnp
from jax import lax
from jax.experimental import pallas as pl
from jax.experimental.pallas import tpu as pltpu
from jax.sharding import PartitionSpec as P

TILE = 128
VMEM_LIMIT = 16 * 1024 * 1024
BIG_LIMIT = 40 * 1024 * 1024
RESIDENT = 16 * 1024 * 1024
BF16 = jnp.bfloat16
F32 = jnp.float32


def full_spec(shape):
    return pl.BlockSpec(shape, lambda *_: (0,) * len(shape))


def params(limit=VMEM_LIMIT):
    return pltpu.CompilerParams(vmem_limit_bytes=limit)


def xor_pairs(size, step):
    return [(i, i ^ step) for i in range(size)]


def z_pairs(pairs):
    return [(2 * a + core, 2 * b + core) for a, b in pairs for core in range(2)]


def densify_kernel(per_piece, per_peer, src_ref, cnt_ref, pos_ref, adj_ref, out_ref, held, sems):
    targets, slots = adj_ref.shape[0], adj_ref.shape[1]
    here = pos_ref[1]
    whole = slots * TILE == out_ref.shape[1]
    copies = [
        pltpu.make_async_copy(adj_ref.at[t], held.at[t], sems.at[t]) for t in range(targets)
    ]
    for copy in copies:
        copy.start()
    for t, copy in enumerate(copies):
        block = ((t // per_peer) ^ pos_ref[0]) * per_peer + t % per_peer
        rows = pl.ds(pl.multiple_of(block * TILE, TILE), TILE)
        if not whole:
            out_ref[rows, :] = jnp.zeros((TILE, out_ref.shape[1]), out_ref.dtype)
        count = cnt_ref[t]
        copy.wait()
        for s in range(slots):
            source = src_ref[t, s]
            slot = (source // per_piece) ^ here
            place = jnp.where((slot == 3) | (slot == 5), slot ^ 6, slot)
            column = pl.multiple_of((place * per_piece + source % per_piece) * TILE, TILE)
            tile = held[t, s]
            out_ref[rows, pl.ds(column, TILE)] = jnp.where(s < count, tile, jnp.zeros_like(tile))


def densify(adjacency, source_tile, tile_count, pos, peers, pieces, capacity):
    targets = adjacency.shape[0]
    width = pieces * capacity
    smem = pl.BlockSpec(memory_space=pltpu.SMEM)
    return pl.pallas_call(
        functools.partial(densify_kernel, capacity // TILE, targets // peers),
        out_shape=jax.ShapeDtypeStruct((targets * TILE, width), BF16),
        in_specs=[smem, smem, smem, pl.BlockSpec(memory_space=pl.ANY)],
        out_specs=pl.BlockSpec(memory_space=pltpu.VMEM),
        scratch_shapes=[
            pltpu.VMEM(adjacency.shape, BF16),
            pltpu.SemaphoreType.DMA((targets,)),
        ],
        compiler_params=params(40 * 1024 * 1024),
        cost_estimate=pl.CostEstimate(
            flops=0, bytes_accessed=4 * targets * TILE * width, transcendentals=0
        ),
        name="densify",
    )(source_tile, tile_count, pos, adjacency)


def densify_blocks_kernel(per_piece, src_ref, cnt_ref, pos_ref, adj_ref, out_ref):
    step = pl.program_id(0)
    tiles, slots = adj_ref.shape[0], adj_ref.shape[1]
    out_ref[...] = jnp.zeros_like(out_ref)
    here = pos_ref[1]
    for t in range(tiles):
        count = cnt_ref[step * tiles + t]
        for s in range(slots):

            @pl.when(s < count)
            def _(t=t, s=s):
                source = src_ref[step * tiles + t, s]
                slot = (source // per_piece) ^ here
                column = pl.multiple_of((slot * per_piece + source % per_piece) * TILE, TILE)
                out_ref[t * TILE : (t + 1) * TILE, pl.ds(column, TILE)] = adj_ref[t, s]


def densify_blocks(adjacency, source_tile, tile_count, pos, pieces, capacity):
    targets, slots = adjacency.shape[0], adjacency.shape[1]
    tiles = 4
    width = pieces * capacity
    return pl.pallas_call(
        functools.partial(densify_blocks_kernel, capacity // TILE),
        out_shape=jax.ShapeDtypeStruct((targets * TILE, width), BF16),
        grid_spec=pltpu.PrefetchScalarGridSpec(
            num_scalar_prefetch=3,
            grid=(targets // tiles,),
            in_specs=[pl.BlockSpec((tiles, slots, TILE, TILE), lambda i, *_: (i, 0, 0, 0))],
            out_specs=pl.BlockSpec((tiles * TILE, width), lambda i, *_: (i, 0)),
        ),
        compiler_params=params(BIG_LIMIT),
        cost_estimate=pl.CostEstimate(
            flops=0, bytes_accessed=2 * targets * TILE * (width + slots * TILE), transcendentals=0
        ),
        name="densify",
    )(source_tile, tile_count, pos, adjacency)


def hits(row, nodes):
    node = lax.broadcasted_iota(jnp.int32, (nodes, row.shape[1]), 0).astype(F32)
    return jnp.where(node == row, 1.0, 0.0).astype(BF16)


def list_row(high, low):
    return high.astype(F32) * 256.0 + low.astype(F32)


def select_kernel(list_ref, pick_ref, put_ref):
    slots, nodes, _ = put_ref.shape
    for slot in range(slots):
        put = hits(list_ref[slot : slot + 1, :], nodes)
        put_ref[slot] = put
        pick_ref[slot] = put.T


def selectors(lists, nodes):
    pieces, capacity = lists.shape
    return pl.pallas_call(
        select_kernel,
        out_shape=(
            jax.ShapeDtypeStruct((pieces, capacity, nodes), BF16),
            jax.ShapeDtypeStruct((pieces, nodes, capacity), BF16),
        ),
        compiler_params=params(BIG_LIMIT),
        cost_estimate=pl.CostEstimate(
            flops=0, bytes_accessed=4 * pieces * capacity * nodes, transcendentals=0
        ),
        name="selectors",
    )(lists)


def gather_rows(sources, here, put_ref, at):
    nodes, capacity = put_ref.shape[1:]
    columns = (sources[0].shape[0] - nodes) // 2
    piece = sources[0][:nodes, :]
    tail = sources[0][nodes:, :].astype(F32)
    for extra in sources[1:]:
        piece = piece + extra[:nodes, :]
        tail = tail + extra[nodes:, :].astype(F32)
    table = list_row(tail[:columns], tail[columns:])
    mine = lax.broadcasted_iota(jnp.int32, table.shape, 0) == here
    put = hits(jnp.sum(jnp.where(mine, table, 0.0), axis=0, keepdims=True), nodes)
    put_ref[at] = put
    rows = lax.dot_general(put, piece, (((0,), (0,)), ((), ())), preferred_element_type=F32)
    return rows.astype(BF16)


def forward_part_kernel(groups, base, peers, added, last, pos_ref, dense_ref, *rest):
    total = sum(groups)
    sources, rest = rest[:total], list(rest[total:])
    before_ref = rest.pop(0) if added else None
    *outs, put_ref, gathered = rest
    here = pos_ref[1]
    capacity = put_ref.shape[2]
    at = 0
    for slot, count in enumerate(groups):
        rows = gather_rows(sources[at : at + count], here, put_ref, slot)
        gathered[slot * capacity : (slot + 1) * capacity, :] = rows
        at += count
    columns = slice(base * capacity, (base + len(groups)) * capacity)
    block = dense_ref.shape[0] // peers
    for peer in range(peers):
        here_rows = slice(peer * block, (peer + 1) * block)
        result = jnp.dot(
            dense_ref[here_rows, columns], gathered[...], preferred_element_type=F32
        )
        if added:
            result = before_ref[here_rows, :] + result
        if last:
            outs[peer][...] = result.astype(outs[peer].dtype)
        else:
            outs[0][here_rows, :] = result


def forward_part(dense, groups, base, pos, peers, nodes, capacity, before=None, last=False):
    rows = dense.shape[0]
    flat = [array for group in groups for array in group]
    width = flat[0].shape[1]
    added = before is not None
    if last:
        outs = tuple(
            jax.ShapeDtypeStruct((rows // peers, width), F32 if peer == 0 else BF16)
            for peer in range(peers)
        )
    else:
        outs = (jax.ShapeDtypeStruct((rows, width), F32),)
    depth = len(groups) * capacity
    if added:
        flat = flat + [before]
    return pl.pallas_call(
        functools.partial(
            forward_part_kernel, tuple(len(group) for group in groups), base, peers, added, last
        ),
        out_shape=outs + (jax.ShapeDtypeStruct((len(groups), nodes, capacity), BF16),),
        in_specs=[pl.BlockSpec(memory_space=pltpu.SMEM)]
        + [pl.BlockSpec(memory_space=pltpu.VMEM)] * (1 + len(flat)),
        scratch_shapes=[pltpu.VMEM((depth, width), BF16)],
        compiler_params=params(),
        cost_estimate=pl.CostEstimate(
            flops=2 * rows * depth * width, bytes_accessed=2 * rows * depth, transcendentals=0
        ),
        name="forward_last" if last else "forward_part",
    )(pos, dense, *flat)


def forward_blocks_kernel(groups, peers, pos_ref, pick_ref, dense_ref, *rest):
    total = sum(groups)
    sources, outs, gathered = rest[:total], rest[total : total + peers], rest[total + peers]
    step = pl.program_id(0)
    capacity = pick_ref.shape[1]

    @pl.when(step == 0)
    def _():
        at = 0
        for slot, count in enumerate(groups):
            piece = sources[at][...]
            for extra in range(1, count):
                piece = piece + sources[at + extra][...]
            at += count
            rows = jnp.dot(pick_ref[slot], piece, preferred_element_type=F32)
            gathered[slot * capacity : (slot + 1) * capacity, :] = rows.astype(BF16)

    result = jnp.dot(dense_ref[...], gathered[...], preferred_element_type=F32)
    for peer in range(peers):

        @pl.when(step == peer)
        def _(peer=peer):
            outs[peer][...] = result.astype(outs[peer].dtype)


def forward_blocks(dense, pick, groups, pos, peers):
    rows, width = dense.shape
    flat = [array for group in groups for array in group]
    nodes, chunk = flat[0].shape
    block = rows // peers
    return pl.pallas_call(
        functools.partial(forward_blocks_kernel, tuple(len(group) for group in groups), peers),
        out_shape=tuple(
            jax.ShapeDtypeStruct((block, chunk), F32 if peer == 0 else BF16)
            for peer in range(peers)
        ),
        grid_spec=pltpu.PrefetchScalarGridSpec(
            num_scalar_prefetch=1,
            grid=(peers,),
            in_specs=[
                full_spec(pick.shape),
                pl.BlockSpec((block, width), lambda i, pos_ref: (i ^ pos_ref[0], 0)),
            ]
            + [full_spec((nodes, chunk))] * len(flat),
            out_specs=tuple(full_spec((block, chunk)) for _ in range(peers)),
            scratch_shapes=[pltpu.VMEM((width, chunk), BF16)],
        ),
        compiler_params=params(BIG_LIMIT),
        cost_estimate=pl.CostEstimate(
            flops=2 * rows * width * chunk, bytes_accessed=2 * rows * width, transcendentals=0
        ),
        name="forward_rows",
    )(pos, pick, dense, *flat)


def layer_kernel(peers, scale, pos_ref, weight_ref, bias_ref, cot_ref, *rest):
    parts, (out_ref, back_ref, mine_ref, theirs_ref) = rest[:peers], rest[peers:]
    total = parts[0][...].astype(F32)
    for peer in range(1, peers):
        total = total + parts[peer][...].astype(F32)
    agg = total.astype(BF16)
    weight = weight_ref[...]
    preact = jnp.dot(agg, weight, preferred_element_type=F32) + bias_ref[...]
    sigma = 1.0 / (1.0 + jnp.exp(-preact))
    out_ref[...] = (preact * sigma).astype(BF16)
    grad = (cot_ref[...].astype(F32) * sigma * (1.0 + preact * (1.0 - sigma))).astype(BF16)
    back_ref[...] = lax.dot_general(
        grad, weight, (((1,), (1,)), ((), ())), preferred_element_type=F32
    ).astype(BF16)
    product = scale * lax.dot_general(
        agg, grad, (((0,), (0,)), ((), ())), preferred_element_type=F32
    )
    bias = scale * jnp.sum(grad.astype(F32).reshape(-1, 8, grad.shape[1]), axis=0)
    half = product.shape[0] // 2
    core = pos_ref[1] % 2
    for keep, give, parity in ((mine_ref, theirs_ref, 0), (theirs_ref, mine_ref, 1)):

        @pl.when(core == parity)
        def _(keep=keep, give=give):
            keep[:half] = product[:half]
            give[:half] = product[half:]

    mine_ref[half:] = bias
    theirs_ref[half:] = bias


def layer(weight, bias_vector, cotangent, parts, pos, scale):
    nodes, width = cotangent.shape
    return pl.pallas_call(
        functools.partial(layer_kernel, len(parts), scale),
        out_shape=(jax.ShapeDtypeStruct((nodes, width), BF16),) * 2
        + (jax.ShapeDtypeStruct((width // 2 + 8, width), F32),) * 2,
        in_specs=[pl.BlockSpec(memory_space=pltpu.SMEM)]
        + [pl.BlockSpec(memory_space=pltpu.VMEM)] * (3 + len(parts)),
        compiler_params=params(),
        cost_estimate=pl.CostEstimate(
            flops=6 * nodes * width * width,
            bytes_accessed=2 * nodes * width * 10,
            transcendentals=nodes * width,
        ),
        name="layer",
    )(pos, weight, bias_vector.reshape(1, -1), cotangent, *parts)


def assemble_kernel(pos_ref, mine_ref, theirs_ref, weight_ref, bias_ref):
    half = weight_ref.shape[0] // 2
    core = pos_ref[1] % 2
    mine = pl.multiple_of(core * half, half)
    theirs = pl.multiple_of((1 - core) * half, half)
    weight_ref[pl.ds(mine, half), :] = mine_ref[:half]
    weight_ref[pl.ds(theirs, half), :] = theirs_ref[:half]
    bias_ref[...] = jnp.sum(mine_ref[half:], axis=0, keepdims=True)


def assemble(mine, theirs, pos):
    width = mine.shape[1]
    weight, bias = pl.pallas_call(
        assemble_kernel,
        out_shape=(
            jax.ShapeDtypeStruct((width, width), F32),
            jax.ShapeDtypeStruct((1, width), F32),
        ),
        in_specs=[pl.BlockSpec(memory_space=pltpu.SMEM)]
        + [pl.BlockSpec(memory_space=pltpu.VMEM)] * 2,
        compiler_params=params(),
        cost_estimate=pl.CostEstimate(
            flops=0, bytes_accessed=16 * width * width, transcendentals=0
        ),
        name="assemble",
    )(pos, mine, theirs)
    return weight, bias.reshape(width)


def back_product(dense, back):
    return lax.dot_general(
        dense, back, (((0,), (0,)), ((), ())), preferred_element_type=F32
    )


def backward_early_kernel(dense_ref, back_ref, out_ref):
    out_ref[...] = back_product(dense_ref[: back_ref.shape[0], :], back_ref[...])


def backward_early(dense, back):
    width, size = dense.shape[1], back.shape[1]
    return pl.pallas_call(
        backward_early_kernel,
        out_shape=jax.ShapeDtypeStruct((width, size), F32),
        compiler_params=params(),
        cost_estimate=pl.CostEstimate(
            flops=2 * width * back.size, bytes_accessed=6 * width * size, transcendentals=0
        ),
        name="backward_early",
    )(dense, back)


def backward_late_kernel(base, slots, peers, dense_ref, *rest):
    puts, rest = rest[: len(slots)], rest[len(slots) :]
    first_ref, rest = rest[0], rest[1:]
    backs, outs, (joined, rows) = rest[: peers - 1], rest[peers - 1 : -2], rest[-2:]
    capacity = puts[0].shape[2]
    block = backs[0].shape[0]
    for peer in range(1, peers):
        joined[(peer - 1) * block : peer * block, :] = backs[peer - 1][...]
    columns = slice(base * capacity, (base + len(outs)) * capacity)
    rows[...] = (
        first_ref[columns, :] + back_product(dense_ref[block:, columns], joined[...])
    ).astype(BF16)
    at = 0
    for put_ref, picked in zip(puts, slots):
        for slot in picked:
            outs[at][...] = jnp.dot(
                put_ref[slot],
                rows[at * capacity : (at + 1) * capacity, :],
                preferred_element_type=F32,
            ).astype(outs[at].dtype)
            at += 1


def backward_late(dense, puts, slots, first, backs, base):
    _, nodes, capacity = puts[0].shape
    count = sum(len(picked) for picked in slots)
    size = first.shape[1]
    return pl.pallas_call(
        functools.partial(backward_late_kernel, base, slots, len(backs) + 1),
        out_shape=tuple(
            jax.ShapeDtypeStruct((nodes, size), BF16 if (base + at) % 2 else F32)
            for at in range(count)
        ),
        scratch_shapes=[
            pltpu.VMEM((len(backs) * backs[0].shape[0], size), BF16),
            pltpu.VMEM((count * capacity, size), BF16),
        ],
        compiler_params=params(),
        cost_estimate=pl.CostEstimate(
            flops=2 * count * capacity * size * dense.shape[0],
            bytes_accessed=2 * dense.shape[0] * count * capacity,
            transcendentals=0,
        ),
        name="backward_late",
    )(dense, *puts, first, *backs)


def backward_blocks_kernel(peers, slots, pos_ref, put_ref, dense_ref, *rest):
    backs, outs, total = rest[:peers], rest[peers : peers + slots], rest[peers + slots]
    step = pl.program_id(0)
    capacity = put_ref.shape[2]
    for peer in range(peers):

        @pl.when(step == peer)
        def _(peer=peer):
            product = lax.dot_general(
                dense_ref[...], backs[peer][...], (((0,), (0,)), ((), ())), preferred_element_type=F32
            )
            if peer == 0:
                total[...] = product
            else:
                total[...] += product

    @pl.when(step == peers - 1)
    def _():
        for slot in range(slots):
            rows = total[slot * capacity : (slot + 1) * capacity, :].astype(BF16)
            outs[slot][...] = jnp.dot(put_ref[slot], rows, preferred_element_type=F32).astype(
                outs[slot].dtype
            )


def backward_blocks(dense, put, backs, pos, kept):
    peers = len(backs)
    rows, width = dense.shape
    slots, nodes, _ = put.shape
    chunk = backs[0].shape[1]
    block = rows // peers
    return pl.pallas_call(
        functools.partial(backward_blocks_kernel, peers, slots),
        out_shape=tuple(
            jax.ShapeDtypeStruct((nodes, chunk), F32 if slot in kept else BF16)
            for slot in range(slots)
        ),
        grid_spec=pltpu.PrefetchScalarGridSpec(
            num_scalar_prefetch=1,
            grid=(peers,),
            in_specs=[
                full_spec(put.shape),
                pl.BlockSpec((block, width), lambda i, pos_ref: (i ^ pos_ref[0], 0)),
            ]
            + [full_spec((block, chunk))] * peers,
            out_specs=tuple(full_spec((nodes, chunk)) for _ in range(slots)),
            scratch_shapes=[pltpu.VMEM((width, chunk), F32)],
        ),
        compiler_params=params(BIG_LIMIT),
        cost_estimate=pl.CostEstimate(
            flops=2 * rows * width * chunk, bytes_accessed=2 * rows * width, transcendentals=0
        ),
        name="backward_rows",
    )(pos, put, dense, *backs)


def pair_sum_kernel(count, *refs):
    for i in range(count):
        total = refs[i][...].astype(F32) + refs[count + i][...].astype(F32)
        refs[2 * count + i][...] = total.astype(refs[2 * count + i].dtype)


def pair_sums(kept, received, wide=-1):
    count = len(kept)
    return pl.pallas_call(
        functools.partial(pair_sum_kernel, count),
        out_shape=tuple(
            jax.ShapeDtypeStruct(kept[i].shape, F32 if i == wide else BF16) for i in range(count)
        ),
        compiler_params=params(),
        cost_estimate=pl.CostEstimate(
            flops=0, bytes_accessed=count * kept[0].size * 8, transcendentals=0
        ),
        name="pair_sums",
    )(*kept, *received)


def triple_sum_kernel(first_ref, second_ref, third_ref, out_ref):
    total = first_ref[...] + second_ref[...].astype(F32) + third_ref[...].astype(F32)
    out_ref[...] = total.astype(BF16)


def triple_sum(first, second, third):
    return pl.pallas_call(
        triple_sum_kernel,
        out_shape=jax.ShapeDtypeStruct(first.shape, BF16),
        compiler_params=params(),
        cost_estimate=pl.CostEstimate(
            flops=0, bytes_accessed=10 * first.size, transcendentals=0
        ),
        name="triple_sum",
    )(first, second, third)


def finish_kernel(chunks, each, *refs):
    out_ref = refs[-1]
    size = out_ref.shape[1] // chunks
    for chunk in range(chunks):
        total = refs[chunk * each][...].astype(F32)
        for term in range(1, each):
            total = total + refs[chunk * each + term][...].astype(F32)
        out_ref[:, chunk * size : (chunk + 1) * size] = total.astype(BF16)


def finish(terms):
    chunks, each = len(terms), len(terms[0])
    nodes, size = terms[0][0].shape
    return pl.pallas_call(
        functools.partial(finish_kernel, chunks, each),
        out_shape=jax.ShapeDtypeStruct((nodes, size * chunks), BF16),
        compiler_params=params(),
        cost_estimate=pl.CostEstimate(
            flops=0, bytes_accessed=chunks * nodes * size * 2 * each, transcendentals=0
        ),
        name="finish",
    )(*[array for group in terms for array in group])


LINE_SWAP1 = z_pairs([(0, 1), (1, 0), (2, 3), (3, 2)])
LINE_SWAP2 = z_pairs([(0, 2), (2, 0), (1, 3), (3, 1)])
LINE_MIDDLE = z_pairs([(1, 2), (2, 1)])
LINE_OUT = z_pairs([(2, 3), (1, 0)])
LINE_IN = z_pairs([(3, 2), (0, 1)])
CORE = xor_pairs(8, 1)


def after(value, *others):
    return lax.optimization_barrier((value,) + others)[0]


def exchange_add(value, axis, size, step):
    return value + lax.ppermute(value, axis, xor_pairs(size, step))


def with_lists(features, list_rows, list_counts):
    live = jnp.arange(list_rows.shape[1])[None, :] < list_counts[:, None]
    high = jnp.where(live, list_rows // 256, -1)
    low = jnp.where(live, list_rows % 256, 0)
    return jnp.concatenate([features, high.astype(BF16), low.astype(BF16)], axis=0)


def line_exchange(piece, dense_of, pos, nodes, capacity, rows):
    far = lax.ppermute(piece, "col", LINE_SWAP2)
    near = lax.ppermute(piece, "col", LINE_SWAP1)
    other = lax.ppermute(piece, "col", CORE)
    dense = dense_of()
    far, dense = lax.optimization_barrier((far, dense))
    ends = lax.ppermute(far, "col", LINE_OUT)
    middle = lax.ppermute(after(piece, far), "col", LINE_MIDDLE)
    early = [[piece], [other], [near], [lax.ppermute(far, "col", CORE)], [far]]
    partial, put_early = forward_part(dense, early, 0, pos, rows, nodes, capacity)
    partial, middle, ends = lax.optimization_barrier((partial, middle, ends))
    other = [lax.ppermute(middle, "col", CORE), lax.ppermute(ends, "col", CORE)]
    late = [[lax.ppermute(near, "col", CORE)], [middle, ends]]
    partial, put_late = forward_part(dense, late, 5, pos, rows, nodes, capacity, partial)
    *blocks, put_last = forward_part(
        dense, [other], 7, pos, rows, nodes, capacity, partial, True
    )
    return dense, (put_early, put_late, put_last), blocks


def row_exchange(own, arrays, rows):
    received = [
        lax.ppermute(arrays[step - 1], "row", xor_pairs(rows, step))
        for step in reversed(range(1, rows))
    ]
    return [own] + received[::-1]


def line_reduce(dense, puts, back, backs, sums, rows, columns):
    put_early, put_late, put_last = puts
    first = backward_early(dense, back)
    sums = sums + after(lax.ppermute(sums, "col", xor_pairs(columns, 4)), backs[2])
    sums = exchange_add(sums, "col", columns, 2)
    *backs, first, sums = lax.optimization_barrier((*backs, first, sums))
    keep3, give3 = backward_late(
        dense, (put_late, put_last), ((1,), (0,)), first, backs, 6
    )
    got3 = lax.ppermute(give3, "col", CORE)
    received = lax.ppermute(sums, "row", xor_pairs(rows, 1))
    keep0, give0, keep1, give2, keep2, give1 = backward_late(
        dense, (put_early, put_late), (tuple(range(5)), (0,)), first, backs, 0
    )
    got3, give2, give1, give0, keep0 = lax.optimization_barrier((got3, give2, give1, give0, keep0))
    (last,) = pair_sums([keep3], [got3])
    passed = lax.ppermute(last, "col", LINE_IN)
    middle = lax.ppermute(last, "col", LINE_MIDDLE)
    got = [lax.ppermute(give, "col", CORE) for give in (give0, give1, give2)]
    own, near = pair_sums([keep0, keep1], got[:2], 0)
    from_near = lax.ppermute(near, "col", LINE_SWAP1)
    sums = sums + after(received, own)
    step = 2
    while step < rows:
        sums = exchange_add(sums, "row", rows, step)
        step *= 2
    far = triple_sum(keep2, got[2], passed)
    from_far = lax.ppermute(far, "col", LINE_SWAP2)
    middle, sums = lax.optimization_barrier((middle, sums))
    sums = after(sums, from_near)
    return [own, middle, from_near, from_far], sums


def per_device(
    features,
    weight,
    bias_vector,
    send_rows,
    send_count,
    adjacency,
    source_tile,
    tile_count,
    cotangent,
):
    rows, columns = lax.axis_size("row"), lax.axis_size("col")
    nodes, width = features.shape
    capacity = send_rows.shape[3]
    tiles, source, count = adjacency[0, 0], source_tile[0, 0], tile_count[0, 0]
    pos = jnp.stack([lax.axis_index("row"), lax.axis_index("col")]).astype(jnp.int32)
    piece = with_lists(features, send_rows[0, 0], send_count[0, 0])
    line = columns == 8 and 2 * tiles.shape[0] * TILE * columns * capacity <= RESIDENT

    if line:
        dense, puts, blocks = line_exchange(
            piece,
            lambda: densify(tiles, source, count, pos, rows, columns, capacity),
            pos,
            nodes,
            capacity,
            rows,
        )
    else:
        dense = densify_blocks(tiles, source, count, pos, columns, capacity)
        pieces = [piece] + [
            lax.ppermute(piece, "col", xor_pairs(columns, step)) for step in range(1, columns)
        ]
        here = lax.axis_index("col")
        lists = jnp.stack(
            [
                list_row(
                    lax.dynamic_index_in_dim(a, nodes + here, 0, keepdims=False),
                    lax.dynamic_index_in_dim(a, nodes + columns + here, 0, keepdims=False),
                )
                for a in pieces
            ]
        )
        pick, put = selectors(lists, nodes)
        blocks = forward_blocks(dense, pick, [[a[:nodes]] for a in pieces], pos, rows)

    parts = row_exchange(blocks[0], blocks[1:], rows)
    scale = 1.0 / math.sqrt(nodes * rows * columns)
    output, back, mine, theirs = layer(weight, bias_vector, cotangent, parts, pos, scale)
    backs = row_exchange(back, [back] * (rows - 1), rows)
    sums = mine + lax.ppermute(theirs, "col", CORE if line else xor_pairs(columns, 1))

    if line:
        terms, sums = line_reduce(
            dense, puts, back, backs[1:], sums, rows, columns
        )
    else:
        scattered = backward_blocks(dense, put, backs, pos, (0,))
        terms = [scattered[0]] + [
            lax.ppermute(scattered[step], "col", xor_pairs(columns, step))
            for step in range(1, columns)
        ]
        step = 2
        while step < columns:
            sums = exchange_add(sums, "col", columns, step)
            step *= 2
        step = 1
        while step < rows:
            sums = exchange_add(sums, "row", rows, step)
            step *= 2
    weight_grad, bias_grad = assemble(
        sums, lax.ppermute(sums, "col", xor_pairs(columns, 1)), pos
    )
    terms[-1], weight_grad, bias_grad = lax.optimization_barrier(
        (terms[-1], weight_grad, bias_grad)
    )
    return output, finish([terms]), weight_grad, bias_grad


def solution(mesh):
    in_specs = (
        P(("row", "col"), None),
        P(),
        P(),
        P("row", "col", None, None),
        P("row", "col", None),
        P("row", "col", None, None, None, None),
        P("row", "col", None, None),
        P("row", "col", None),
        P(("row", "col"), None),
    )
    out_specs = (P(("row", "col"), None), P(("row", "col"), None), P(), P())
    return jax.shard_map(
        per_device, mesh=mesh, in_specs=in_specs, out_specs=out_specs, check_vma=False
    )
```
